32 devices in a mesh: dp: 4 (over x, core), tensor: 8 (over z, y).
Axes of the slice: x: 2, y: 2, z: 4, core: 2. Of those that a mesh axis runs over, the one named last changes fastest.
Arguments:
- activations: bfloat16 [4, 2048, 512], P('dp', 'tensor'), may hold values from -6 to 6
- out_grad: bfloat16 [4, 2048, 28672], P('dp', None, 'tensor'), may hold values from -0.125 to 0.125
- residual: float32 [4, 512, 28672], P('dp', None, 'tensor'), may hold values from -4 to 4
- chosen: int32 [4, 8, 896], P(None, 'tensor'), may hold values from 0 to 3583, as said below
- master: float32 [512, 28672], P('dp', 'tensor'), may hold values from -6 to 6
- moment_one: float32 [512, 28672], P('dp', 'tensor'), may hold values from -4 to 4
- moment_two: float32 [512, 28672], P('dp', 'tensor'), may hold values from 0.01 to 1
- params: bfloat16 [512, 28672], P(None, 'tensor'), may hold values from -6 to 6
Outputs:
- new_residual: float32 [4, 512, 28672], P('dp', None, 'tensor')
- new_moment_one: float32 [512, 28672], P('dp', 'tensor')
- new_moment_two: float32 [512, 28672], P('dp', 'tensor')
- new_master: float32 [512, 28672], P('dp', 'tensor')
- new_params: bfloat16 [512, 28672], P(None, 'tensor')
The draws below stay inside these ranges and needn't reach their ends.
Inputs may be any that keep to these rules, and one draw needn't show every extreme that they name: For each owner o and column shard t, chosen[o, t] holds 896 distinct span numbers of that owner's rows and that shard's columns, the same for every replica.
All inputs are finite; a program needn't handle non-finite values.
Results may differ from the reference program's by a relative error of at most 0.001.
Values may be sent and summed in bfloat16 or wider, within the bound.
No kernel may reach another device: no remote copies, remote signals or barrier semaphores. Data moves between devices by JAX's collectives and lax.ppermute only.
A program may use at most 128 MiB of HBM per device.

```python
import math
import jax
import jax.numpy as jnp
from jax import lax

FF = 28672
ROWS = 512
SPAN = 128
TOKENS = 2048
CHOSEN = 896
N_DP = 4
N_TENSOR = 8


def draw_chosen(key, part):
    per_owner = ROWS // N_DP * (FF // (SPAN * N_TENSOR))
    group_keys = jax.random.split(key, N_DP * N_TENSOR)
    group_index = jnp.arange(N_DP * N_TENSOR, dtype=jnp.int32)

    def draw_group(group_key, position):
        first_key, second_key, third_key = jax.random.split(group_key, 3)
        middle = jax.random.permutation(first_key, per_owner - 2)[:CHOSEN - 2] + 1
        listed = jnp.concatenate([middle.astype(jnp.int32), jnp.array([0, per_owner - 1], jnp.int32)])
        listed = listed[jax.random.permutation(second_key, CHOSEN)]
        loose = jax.random.permutation(third_key, per_owner)[:CHOSEN].astype(jnp.int32)
        return jnp.where(position == 0, listed, loose)
    return jax.vmap(draw_group)(group_keys, group_index).reshape(N_DP, N_TENSOR, CHOSEN).astype(jnp.int32)


def shard_levels(key, dims, cuts, smallest, high):
    level, own = 1.0, jax.random.fold_in(key, 6)
    for dim, parts in cuts:
        heights = jnp.exp(jax.random.uniform(jax.random.fold_in(own, dim), (parts,), jnp.float32, smallest / len(cuts), high / len(cuts)))
        level = level * jnp.repeat(heights, dims[dim] // parts).reshape([-1 if axis == dim else 1 for axis in range(len(dims))])
    return level


def scatter_about(stream_key, shape, spread, limit, cuts=(), kind=jnp.bfloat16):
    values = spread * jax.random.normal(stream_key, shape, jnp.float32)
    if cuts:
        values = values * shard_levels(stream_key, shape, cuts, -0.22, 0.18)
    return jnp.clip(values, -limit, limit).astype(kind)


def setup_inputs(seed: int = 0) -> dict:
    keys = jax.random.split(jax.random.key(seed), 9)
    return {
        "activations": scatter_about(keys[0], (N_DP, TOKENS, ROWS), 1.0, 6.0, ((0, 4), (1, 8))),
        "out_grad": scatter_about(keys[1], (N_DP, TOKENS, FF), TOKENS ** -0.5, 0.125, ((0, 4), (2, 8))),
        "residual": scatter_about(keys[2], (N_DP, ROWS, FF), 0.5, 4.0, ((0, 4), (2, 8)), jnp.float32),
        "chosen": draw_chosen(jax.random.fold_in(keys[8], 71), 0),
        "master": scatter_about(keys[4], (ROWS, FF), 1.0, 6.0, ((0, 4), (1, 8)), jnp.float32),
        "moment_one": scatter_about(keys[5], (ROWS, FF), 0.5, 4.0, ((0, 4), (1, 8)), jnp.float32),
        "moment_two": jnp.clip(jnp.exp(math.log(1.0) - 4.6051702 * jax.random.uniform(keys[6], (ROWS, FF), jnp.float32) ** shard_levels(keys[6], (ROWS, FF), ((0, 4), (1, 8)), -0.2, 0.2)), 0.01, 1.0),
        "params": scatter_about(keys[7], (ROWS, FF), 1.0, 6.0, ((1, 8),)),
    }


beta_one = 0.9
beta_two = 0.999
learn_rate = 0.01
decay_rate = 0.1
epsilon = 1e-08

def replica_grad(pair):
    return jnp.dot(pair[0].astype(jnp.float32).T, pair[1].astype(jnp.float32), precision=lax.Precision.HIGHEST)

def reference(activations, out_grad, residual, chosen, master, moment_one, moment_two, params):
    weight_grad = lax.map(replica_grad, (activations, out_grad))
    accumulated = residual + weight_grad
    owner_rows = ROWS // N_DP
    per_row = FF // (SPAN * N_TENSOR)
    per_owner = owner_rows * per_row
    owner_ids = jnp.arange(N_DP, dtype=jnp.int32)[:, None, None]
    tensor_ids = jnp.arange(N_TENSOR, dtype=jnp.int32)[None, :, None]
    flags = jnp.zeros((N_DP, N_TENSOR, per_owner), jnp.float32).at[owner_ids, tensor_ids, chosen].set(1.0)
    flags = flags.reshape(N_DP, N_TENSOR, owner_rows, per_row).transpose(0, 2, 1, 3).reshape(ROWS, FF // SPAN)
    chosen_mask = jnp.repeat(flags, SPAN, axis=1)
    new_residual = accumulated * (1.0 - chosen_mask)
    mean_grad = lax.optimization_barrier(jnp.sum(accumulated, axis=0)) / N_DP
    picked = chosen_mask > 0.5
    moment_next = beta_one * moment_one + (1.0 - beta_one) * mean_grad
    second_next = beta_two * moment_two + (1.0 - beta_two) * mean_grad * mean_grad
    master_next = master - learn_rate * (moment_next / (jnp.sqrt(second_next) + epsilon) + decay_rate * master)
    new_moment_one = jnp.where(picked, moment_next, moment_one)
    new_moment_two = jnp.where(picked, second_next, moment_two)
    new_master = jnp.where(picked, master_next, master)
    new_params = jnp.where(picked, master_next.astype(jnp.bfloat16), params)
    return (new_residual, new_moment_one, new_moment_two, new_master, new_params)
```

```python
import functools
import jax
import jax.numpy as jnp
import numpy as np
from jax import lax
from jax.experimental import pallas as pl
from jax.experimental.pallas import tpu as pltpu
from jax.sharding import PartitionSpec as P

beta_one = 0.9
beta_two = 0.999
learn_rate = 0.01
decay_rate = 0.1
epsilon = 1e-08
LANES = 128
SUBLANES = 8
UNROLL = 16


def ring_order(count):
    inner = 4 if count % 16 == 0 else 2
    outer = count // inner
    cells = []
    for row in range(outer):
        steps = range(1, inner) if row % 2 == 0 else range(inner - 1, 0, -1)
        cells += [row * inner + step for step in steps]
    return cells + [row * inner for row in range(outer - 1, -1, -1)]


def plan_table(dp_count, tensor_count):
    ring = ring_order(tensor_count)
    place = {cell: i for i, cell in enumerate(ring)}
    chips = dp_count // 2
    table = np.zeros((dp_count, tensor_count, tensor_count + dp_count), np.int32)
    for d in range(dp_count):
        owners = [((d // 2 + k) % chips) * 2 + ((d % 2) ^ j) for k in range(chips) for j in range(2)]
        for t in range(tensor_count):
            table[d, t, :tensor_count] = [ring[(place[t] + j) % tensor_count] for j in range(tensor_count)]
            table[d, t, tensor_count:] = owners
    return table


def tiles(values):
    rows, columns = values.shape
    split = values.reshape(rows // SUBLANES, SUBLANES, columns // LANES, LANES)
    return split.transpose(0, 2, 1, 3).reshape(rows * columns // LANES, LANES)


def untiles(values, rows, columns):
    split = values.reshape(rows // SUBLANES, columns // LANES, SUBLANES, LANES)
    return split.transpose(0, 2, 1, 3).reshape(rows, columns)


def params_of(limit_mib):
    return pltpu.CompilerParams(vmem_limit_bytes=limit_mib << 20)


def whole(shape):
    return pl.BlockSpec(shape, lambda i, *_: (0,) * len(shape))


def each_row(count, body):
    def step(i, carry):
        for k in range(UNROLL):
            body(i * UNROLL + k)
        return carry

    lax.fori_loop(0, count // UNROLL, step, 0)


def accumulate_body(chunk_count, plan_ref, base_ref, *refs):
    total = base_ref[...]
    for j in range(chunk_count):
        total = total + lax.dot_general(
            refs[j][...], refs[chunk_count + j][...], (((0,), (0,)), ((), ())), preferred_element_type=jnp.float32
        )
    refs[-1][...] = total


def accumulate(plan, base, chunks, places, token_grad):
    rows, columns = base.shape
    tokens = chunks[0].shape[0]
    width = columns // 7
    grad_specs = [pl.BlockSpec((tokens, width), lambda i, plan, j=j: (plan[j], i)) for j in places]
    return pl.pallas_call(
        functools.partial(accumulate_body, len(chunks)),
        out_shape=jax.ShapeDtypeStruct(base.shape, jnp.float32),
        grid_spec=pltpu.PrefetchScalarGridSpec(
            num_scalar_prefetch=1,
            grid=(columns // width,),
            in_specs=[pl.BlockSpec((rows, width), lambda i, plan: (0, i))]
            + [whole((tokens, rows))] * len(chunks)
            + grad_specs,
            out_specs=pl.BlockSpec((rows, width), lambda i, plan: (0, i)),
        ),
        cost_estimate=pl.CostEstimate(
            flops=2 * rows * columns * tokens * len(chunks),
            bytes_accessed=8 * rows * columns + 2 * tokens * columns * len(chunks),
            transcendentals=0,
        ),
        compiler_params=params_of(24),
        name="accumulate",
    )(plan, base, *chunks, *([token_grad] * len(chunks)))


def finish_body(sizes, first, plan_ref, ids_ref, base_ref, front_ref, back_ref, grad_ref, *refs):
    per_owner, owner_rows, count, place = sizes
    out_ref, packed_ref, rows_ref, part_ref = refs[-4:]
    half, columns = front_ref.shape[0], grad_ref.shape[1]
    owner = plan_ref[place]
    blocks = columns // LANES
    wide = 2 * LANES
    offset = pl.multiple_of(lax.rem(owner * owner_rows, front_ref.shape[1]), SUBLANES)
    for start in range(0, columns, wide):
        part = lax.dot_general(
            front_ref[...], grad_ref[:half, start : start + wide], (((0,), (0,)), ((), ())), preferred_element_type=jnp.float32
        ) + lax.dot_general(
            back_ref[...], grad_ref[half:, start : start + wide], (((0,), (0,)), ((), ())), preferred_element_type=jnp.float32
        )
        if front_ref.shape[1] != owner_rows:
            part_ref[...] = part
            part = part_ref[pl.ds(offset, owner_rows), :]
        for r in range(owner_rows // SUBLANES):
            for c in range(wide // LANES):
                at = (r * blocks + start // LANES + c) * SUBLANES
                out_ref[at : at + SUBLANES, :] = (
                    base_ref[at : at + SUBLANES, :]
                    + part[r * SUBLANES : (r + 1) * SUBLANES, c * LANES : (c + 1) * LANES]
                )
    zero = jnp.zeros((1, LANES), jnp.float32)
    begin = owner * count

    def move(i):
        at = ids_ref[begin + i]
        rows_ref[pl.ds(i, 1), :] = out_ref[pl.ds(at, 1), :]
        out_ref[pl.ds(at, 1), :] = zero

    each_row(count, move)
    packed_ref[...] = rows_ref[...].astype(packed_ref.dtype)


def finish(plan, ids, base, front, back, token_grad, residual, place, origin, count, kind):
    dp_count = ids.shape[0] // count
    per_owner = base.shape[0] // dp_count
    half, rows = front.shape
    owner_rows = rows // dp_count
    columns = token_grad.shape[1]
    lanes = max(LANES, owner_rows)
    ratio = lanes // owner_rows
    first = residual is None
    operands = [plan, ids, base, front, back, token_grad]
    in_specs = [
        pl.BlockSpec((per_owner, LANES), lambda i, plan, ids: (plan[place], 0)),
        pl.BlockSpec((half, lanes), lambda i, plan, ids: (0, plan[place] // ratio)),
        pl.BlockSpec((half, lanes), lambda i, plan, ids: (0, plan[place] // ratio)),
        pl.BlockSpec((2 * half, columns), lambda i, plan, ids: (plan[origin], 0)),
    ]
    aliases = {}
    if not first:
        aliases = {len(operands): 0}
        operands.append(residual)
        in_specs.append(pl.BlockSpec(memory_space=pl.ANY))
    return pl.pallas_call(
        functools.partial(finish_body, (per_owner, owner_rows, count, place), first),
        out_shape=[jax.ShapeDtypeStruct(base.shape, jnp.float32), jax.ShapeDtypeStruct((count, LANES), kind)],
        grid_spec=pltpu.PrefetchScalarGridSpec(
            num_scalar_prefetch=2,
            grid=(1,),
            in_specs=in_specs,
            out_specs=[
                pl.BlockSpec((per_owner, LANES), lambda i, plan, ids: (plan[place], 0)),
                whole((count, LANES)),
            ],
            scratch_shapes=[pltpu.VMEM((count, LANES), jnp.float32), pltpu.VMEM((lanes, 2 * LANES), jnp.float32)],
        ),
        input_output_aliases=aliases,
        cost_estimate=pl.CostEstimate(
            flops=4 * half * per_owner * LANES + 5000 * count * LANES,
            bytes_accessed=8 * per_owner * LANES + 4 * half * columns,
            transcendentals=0,
        ),
        compiler_params=params_of(24),
        name="finish",
    )(*operands)


def fetch_body(count, place, plan_ref, ids_ref, one_ref, two_ref, master_ref, *outs):
    begin = plan_ref[place] * count

    def move(i):
        at = ids_ref[begin + i]
        for source, target in zip((one_ref, two_ref, master_ref), outs):
            target[pl.ds(i, 1), :] = source[pl.ds(at, 1), :]

    each_row(count, move)


def fetch(plan, ids, states, place, count):
    size = states[0].shape
    return pl.pallas_call(
        functools.partial(fetch_body, count, place),
        out_shape=[jax.ShapeDtypeStruct((count, LANES), jnp.float32)] * 3,
        grid_spec=pltpu.PrefetchScalarGridSpec(
            num_scalar_prefetch=2,
            grid=(1,),
            in_specs=[whole(size)] * 3,
            out_specs=[whole((count, LANES))] * 3,
        ),
        cost_estimate=pl.CostEstimate(flops=0, bytes_accessed=12 * size[0] * LANES, transcendentals=0),
        compiler_params=params_of(24),
        name="fetch",
    )(plan, ids, *states)


def store_body(count, place, plan_ref, ids_ref, *refs):
    old, new, outs = refs[:3], refs[3:6], refs[6:]
    begin = plan_ref[place] * count
    for source, target in zip(old, outs):
        target[...] = source[...]

    def move(i):
        at = ids_ref[begin + i]
        for source, target in zip(new, outs):
            target[pl.ds(at, 1), :] = source[pl.ds(i, 1), :]

    each_row(count, move)


def store(plan, ids, states, updates, place, count):
    size = states[0].shape
    return pl.pallas_call(
        functools.partial(store_body, count, place),
        out_shape=[jax.ShapeDtypeStruct(size, jnp.float32)] * 3,
        grid_spec=pltpu.PrefetchScalarGridSpec(
            num_scalar_prefetch=2,
            grid=(1,),
            in_specs=[whole(size)] * 3 + [whole((count, LANES))] * 3,
            out_specs=[whole(size)] * 3,
        ),
        cost_estimate=pl.CostEstimate(flops=0, bytes_accessed=24 * size[0] * LANES, transcendentals=0),
        compiler_params=params_of(32),
        name="store",
    )(plan, ids, *states, *updates)


def spread_body(count, place, plan_ref, ids_ref, params_ref, update_ref, *refs):
    out_ref, dense_ref, rows_ref = refs[-3:]
    begin = plan_ref[place] * count
    dense_ref[...] = params_ref[...].astype(jnp.float32)
    rows_ref[...] = update_ref[...].astype(jnp.float32)

    def move(i):
        at = ids_ref[begin + i]
        dense_ref[pl.ds(at, 1), :] = rows_ref[pl.ds(i, 1), :]

    each_row(count, move)
    out_ref[...] = dense_ref[...].astype(out_ref.dtype)


def spread(plan, ids, weights, update, earlier, place, count):
    dp_count = ids.shape[0] // count
    per_owner = weights.shape[0] // dp_count
    operands = [plan, ids, weights, update]
    mine = pl.BlockSpec((per_owner, LANES), lambda i, plan, ids: (plan[place], 0))
    in_specs = [mine, whole((count, LANES))]
    aliases = {}
    if earlier is not None:
        aliases = {len(operands): 0}
        operands.append(earlier)
        in_specs.append(pl.BlockSpec(memory_space=pl.ANY))
    return pl.pallas_call(
        functools.partial(spread_body, count, place),
        out_shape=jax.ShapeDtypeStruct(weights.shape, weights.dtype),
        grid_spec=pltpu.PrefetchScalarGridSpec(
            num_scalar_prefetch=2,
            grid=(1,),
            in_specs=in_specs,
            out_specs=mine,
            scratch_shapes=[pltpu.VMEM((per_owner, LANES), jnp.float32), pltpu.VMEM((count, LANES), jnp.float32)],
        ),
        input_output_aliases=aliases,
        cost_estimate=pl.CostEstimate(
            flops=0, bytes_accessed=12 * per_owner * LANES, transcendentals=0
        ),
        compiler_params=params_of(24),
        name="spread",
    )(*operands)


def local(table, ring, activations, out_grad, residual, chosen, master, moment_one, moment_two, params):
    token_grad = out_grad[0]
    own = activations[0]
    tokens, row_count = own.shape
    column_count = token_grad.shape[1]
    dp_count, tensor_count = table.shape[:2]
    chips = dp_count // 2
    owner_rows = row_count // dp_count
    count = chosen.shape[2]
    blocks = column_count // LANES

    plan = jnp.asarray(table)[lax.axis_index("dp"), lax.axis_index("tensor")]
    spans = chosen[:, 0, :]
    row, column = spans // blocks, spans % blocks
    ids = ((row // SUBLANES * blocks + column) * SUBLANES + row % SUBLANES).reshape(-1)

    ahead = [(ring[i], ring[(i + 1) % tensor_count]) for i in range(tensor_count)]
    behind = [(b, a) for a, b in ahead]

    states = [tiles(v) for v in (moment_one, moment_two, master)]
    place_of = lambda k, j: tensor_count + 2 * k + j
    own_place = place_of(0, 0)

    total = accumulate(plan, residual[0], [own], [0], token_grad)
    front = back = own
    for hop in range(1, tensor_count // 2):
        front = lax.ppermute(front, "tensor", ahead)
        back = lax.ppermute(back, "tensor", behind)
        total = accumulate(plan, total, [front, back], [tensor_count - hop, hop], token_grad)
    front = lax.ppermute(front[: tokens // 2], "tensor", ahead)
    back = lax.ppermute(back[tokens // 2 :], "tensor", behind)

    picked = fetch(plan, ids, states, own_place, count)
    total = tiles(total)
    left = None

    def close(left, k, j, kind):
        return finish(
            plan, ids, total, front, back, token_grad, left, place_of(k, j), tensor_count // 2, count, kind
        )

    def swap(values):
        return lax.ppermute(values, "dp", [(d, d ^ 1) for d in range(dp_count)])

    def send(values, k):
        return lax.ppermute(
            values, "dp", [(d, ((d // 2 + k) % chips) * 2 + d % 2) for d in range(dp_count)]
        )

    received = []
    for k in range(1, chips):
        left, other = close(left, k, 1, jnp.bfloat16)
        other = swap(other)
        left, mine = close(left, k, 0, jnp.float32)
        received.append(send((mine + other.astype(jnp.float32)).astype(jnp.bfloat16), k))
    left, other = close(left, 0, 1, jnp.bfloat16)
    received.append(swap(other))
    left, mine = close(left, 0, 0, jnp.float32)
    for part in received:
        mine = mine + part.astype(jnp.float32)
    mean_grad = mine / dp_count

    one, two, weights = picked
    one = beta_one * one + (1.0 - beta_one) * mean_grad
    two = beta_two * two + (1.0 - beta_two) * mean_grad * mean_grad
    weights = weights - learn_rate * (one / (jnp.sqrt(two) + epsilon) + decay_rate * weights)
    rounded = weights.astype(jnp.bfloat16)

    far = [send(rounded, k) for k in range(1, chips)]
    near = swap(rounded)
    fresh = store(plan, ids, states, [one, two, weights], own_place, count)
    flat = tiles(params)
    out = spread(plan, ids, flat, rounded, None, own_place, count)
    out = spread(plan, ids, flat, near, out, place_of(0, 1), count)
    for k in range(1, chips):
        across = swap(far[k - 1])
        out = spread(plan, ids, flat, far[k - 1], out, place_of(chips - k, 0), count)
        out = spread(plan, ids, flat, across, out, place_of(chips - k, 1), count)

    new_one, new_two, new_master = (untiles(v, owner_rows, column_count) for v in fresh)
    return (
        untiles(left, row_count, column_count)[None],
        new_one,
        new_two,
        new_master,
        untiles(out, row_count, column_count),
    )


def solution(mesh):
    dp_count, tensor_count = mesh.shape["dp"], mesh.shape["tensor"]
    body = functools.partial(local, plan_table(dp_count, tensor_count), ring_order(tensor_count))
    in_specs = (
        P("dp", "tensor", None),
        P("dp", None, "tensor"),
        P("dp", None, "tensor"),
        P(None, "tensor", None),
        P("dp", "tensor"),
        P("dp", "tensor"),
        P("dp", "tensor"),
        P(None, "tensor"),
    )
    out_specs = (
        P("dp", None, "tensor"),
        P("dp", "tensor"),
        P("dp", "tensor"),
        P("dp", "tensor"),
        P(None, "tensor"),
    )
    return jax.shard_map(body, mesh=mesh, in_specs=in_specs, out_specs=out_specs, check_vma=False)
```

```python
import functools
import jax
import jax.numpy as jnp
import numpy as np
from jax import lax
from jax.experimental import pallas as pl
from jax.experimental.pallas import tpu as pltpu
from jax.sharding import PartitionSpec as P

beta_one = 0.9
beta_two = 0.999
learn_rate = 0.01
decay_rate = 0.1
epsilon = 1e-08
LANES = 128
SUBLANES = 8
UNROLL = 16


def ring_order(count):
    inner = 4 if count % 16 == 0 else 2
    outer = count // inner
    cells = []
    for row in range(outer):
        steps = range(1, inner) if row % 2 == 0 else range(inner - 1, 0, -1)
        cells += [row * inner + step for step in steps]
    return cells + [row * inner for row in range(outer - 1, -1, -1)]


def plan_table(dp_count, tensor_count):
    ring = ring_order(tensor_count)
    place = {cell: i for i, cell in enumerate(ring)}
    chips = dp_count // 2
    table = np.zeros((dp_count, tensor_count, tensor_count + dp_count), np.int32)
    for d in range(dp_count):
        owners = [((d // 2 + k) % chips) * 2 + ((d % 2) ^ j) for k in range(chips) for j in range(2)]
        for t in range(tensor_count):
            table[d, t, :tensor_count] = [ring[(place[t] + j) % tensor_count] for j in range(tensor_count)]
            table[d, t, tensor_count:] = owners
    return table


def tiles(values):
    rows, columns = values.shape
    split = values.reshape(rows // SUBLANES, SUBLANES, columns // LANES, LANES)
    return split.transpose(0, 2, 1, 3).reshape(rows * columns // LANES, LANES)


def untiles(values, rows, columns):
    split = values.reshape(rows // SUBLANES, columns // LANES, SUBLANES, LANES)
    return split.transpose(0, 2, 1, 3).reshape(rows, columns)


VMEM = pltpu.MemorySpace.VMEM
HELD = pl.BlockSpec(memory_space=VMEM)
AWAY = pl.BlockSpec(memory_space=pl.ANY)
DMA = pltpu.SemaphoreType.DMA
WIDTH = 896
WEIGHT = 24


def each_group(count, body):
    def step(i, carry):
        body([i * UNROLL + k for k in range(UNROLL)])
        return carry

    lax.fori_loop(0, count // UNROLL, step, 0)


def gather_rows(look, count, pairs):
    def move(rows):
        at = [look(i) for i in rows]
        for source, target in pairs:
            values = [source[pl.ds(a, 1), :] for a in at]
            for i, value in zip(rows, values):
                target[pl.ds(i, 1), :] = value

    each_group(count, move)


def scatter_rows(look, count, pairs):
    def move(rows):
        at = [look(i) for i in rows]
        for source, target in pairs:
            values = [source[pl.ds(i, 1), :] for i in rows]
            for a, value in zip(at, values):
                target[pl.ds(a, 1), :] = value

    each_group(count, move)


def product(a, b):
    return lax.dot_general(a, b, (((0,), (0,)), ((), ())), preferred_element_type=jnp.float32)


def add_products(total_in, total_out, grad_ref, terms):
    columns = grad_ref.shape[1]
    width = WIDTH if columns % WIDTH == 0 else LANES

    def step(i, carry):
        at = pl.ds(pl.multiple_of(i * width, LANES), width)
        total = total_in[:, at]
        for chunk, start in terms:
            total = total + product(chunk[...], grad_ref[pl.ds(start, chunk.shape[0]), at])
        total_out[:, at] = total
        return carry

    lax.fori_loop(0, columns // width, step, 0)


def split_copies(source, target, parts, sems, first=0):
    size = source.shape[0] // parts
    return [
        pltpu.make_async_copy(source.at[pl.ds(k * size, size)], target.at[pl.ds(k * size, size)], sems.at[first + k])
        for k in range(parts)
    ]


def start_all(copies):
    for copy in copies:
        copy.start()


def wait_all(copies):
    for copy in copies:
        copy.wait()


def away(values):
    return pltpu.with_memory_space_constraint(values, pltpu.MemorySpace.HBM)


def call(body, name, scalars, operands, outs, scratch=(), aliases=None, flops=0, traffic=0):
    return pl.pallas_call(
        body,
        out_shape=[
            pltpu.VMEM(shape, kind) if held else jax.ShapeDtypeStruct(shape, kind) for shape, kind, held in outs
        ],
        grid_spec=pltpu.PrefetchScalarGridSpec(
            num_scalar_prefetch=len(scalars),
            grid=(1,),
            in_specs=[held if isinstance(held, pl.BlockSpec) else HELD if held else AWAY for _, held in operands],
            out_specs=[HELD if held else AWAY for _, _, held in outs],
            scratch_shapes=list(scratch),
        ),
        input_output_aliases={len(scalars) + k: v for k, v in (aliases or {}).items()},
        cost_estimate=pl.CostEstimate(flops=flops, bytes_accessed=traffic, transcendentals=0),
        compiler_params=pltpu.CompilerParams(vmem_limit_bytes=6 << 20),
        name=name,
    )(*scalars, *(values for values, _ in operands))


def look_in(ids_ref):
    return lambda i: ids_ref[0, i]


def look_from(ids_ref, per_owner, count):
    begin = ids_ref[0, count] * per_owner
    return lambda i: ids_ref[0, i] - begin


def ids_of(ids, place):
    return ids, pl.BlockSpec((None, *ids.shape[1:]), lambda i, *_: (place, 0, 0), memory_space=pltpu.SMEM)


def order_ids(plan_ref, spans_ref, ids_ref, columns, rows):
    dp_count, _, count = spans_ref.shape
    blocks = columns // LANES
    per_owner = rows // dp_count * blocks
    factor = -(-(1 << 18) // blocks)
    assert per_owner * (factor * blocks - (1 << 18)) < 1 << 18
    for p in range(dp_count):
        owner = plan_ref[plan_ref.shape[0] - dp_count + p]
        spans = spans_ref[owner]
        row = lax.shift_right_logical(spans * factor, 18)
        column = spans - row * blocks
        tile = lax.shift_right_logical(row, 3) * blocks + column
        ids_ref[p, :, :count] = tile * SUBLANES + (row & 7) + owner * per_owner
        ids_ref[p, :, count:] = jnp.full((1, LANES), 1, jnp.int32) * owner


def grad_copies(plan_ref, places, tokens, grad_ref, held_ref, sems, first=0):
    half, copies = tokens // 2, []
    for n, j in enumerate(places):
        for k in range(2):
            at = pl.ds(pl.multiple_of(plan_ref[j] * tokens + k * half, half), half)
            copies.append(pltpu.make_async_copy(grad_ref.at[at], held_ref.at[at], sems.at[first + 2 * n + k]))
    return copies


def load_body(
    places, plan_ref, residual_ref, grad_ref, own_ref, spans_ref, total_ref, held_ref, ids_ref, own_held, spans_held, sems, own_sems
):
    tokens = own_ref.shape[0]
    spans_copy = pltpu.make_async_copy(spans_ref, spans_held, own_sems.at[1])
    spans_copy.start()
    first = [pltpu.make_async_copy(own_ref, own_held, own_sems.at[0])]
    first += grad_copies(plan_ref, [0], tokens, grad_ref, held_ref, sems, 8)
    first += split_copies(residual_ref, total_ref, 8, sems)
    later = grad_copies(plan_ref, places, tokens, grad_ref, held_ref, sems, 10)
    start_all(first)
    spans_copy.wait()
    order_ids(plan_ref, spans_held, ids_ref, total_ref.shape[1], total_ref.shape[0])
    wait_all(first)
    start_all(later)
    add_products(total_ref, total_ref, held_ref, [(own_held, pl.multiple_of(plan_ref[0] * tokens, tokens))])
    wait_all(later)


def load(plan, residual, token_grad, own, spans, places):
    return call(
        functools.partial(load_body, places),
        "load",
        [plan],
        [(away(residual), False), (away(token_grad), False), (away(own), False), (away(spans), False)],
        [
            (residual.shape, jnp.float32, True),
            (token_grad.shape, token_grad.dtype, True),
            ((*spans.shape[:2], spans.shape[2] + LANES), jnp.int32, True),
        ],
        [
            pltpu.VMEM(own.shape, own.dtype),
            pltpu.VMEM(spans.shape, jnp.int32),
            DMA((10 + 2 * len(places),)),
            DMA((2,)),
        ],
        flops=WEIGHT * own.size * residual.shape[1],
        traffic=WEIGHT * residual.size,
    )


def accumulate_body(places, coming, tokens, side, plan_ref, total_in, held_in, grad_ref, *refs):
    chunks, refs = refs[: len(places)], refs[len(places) :]
    starts = [pl.multiple_of(plan_ref[j] * tokens, tokens) for j in places]
    extra = {"states": 3, "params": 1, "pick": 4}.get(side, 0)
    sources, (total_out, held_ref), refs = refs[:extra], refs[extra : extra + 2], refs[extra + 2 :]
    sems = refs[-1]
    copies = grad_copies(plan_ref, coming, tokens, grad_ref, held_ref, sems, 6)
    if side == "states":
        helds = refs[:3]
        copies += [c for n in range(3) for c in split_copies(sources[n], helds[n], 2, sems, 2 * n)]
    if side == "params":
        wide_ref, narrow_ref = refs[:2]
        copies += split_copies(sources[0], narrow_ref, 4, sems)
    start_all(copies)
    add_products(total_in, total_out, held_ref, list(zip(chunks, starts)))
    wait_all(copies)
    if side == "pick":
        count = refs[0].shape[0]
        gather_rows(look_from(sources[3], sources[0].shape[0], count), count, list(zip(sources[:3], refs[:3])))
    if side == "params":
        wide_ref[...] = narrow_ref[...].astype(jnp.float32)


def accumulate(plan, total, chunks, places, held_grad, token_grad, coming, side=None, sources=()):
    tokens = chunks[0].shape[0]
    outs, scratch = [(total.shape, jnp.float32, True), (held_grad.shape, held_grad.dtype, True)], []
    inputs = []
    if side == "states":
        inputs = [(away(v), False) for v in sources]
        outs += [(sources[0].shape, jnp.float32, True)] * 3
    if side == "pick":
        count = sources[3][0].shape[2] - LANES
        inputs = [(v, True) for v in sources[:3]] + [sources[3]]
        outs += [((count, LANES), jnp.float32, True)] * 3
    if side == "params":
        inputs = [(away(sources[0]), False)]
        outs += [(sources[0].shape, jnp.float32, True)]
        scratch = [pltpu.VMEM(sources[0].shape, sources[0].dtype)]
    return call(
        functools.partial(accumulate_body, places, coming, tokens, side),
        "accumulate",
        [plan],
        [(total, True), (held_grad, True), (away(token_grad), False)] + [(c, True) for c in chunks] + inputs,
        outs,
        scratch + [DMA((6 + 2 * len(coming),))],
        {0: 0, 1: 1},
        flops=WEIGHT * tokens * total.size * len(chunks),
        traffic=WEIGHT * total.size,
    )


def last_body(place, plan_ref, total_in, grad_ref, front_ref, back_ref, total_out, chunk_ref):
    half = front_ref.shape[0]
    chunk_ref[:half] = front_ref[...]
    chunk_ref[half:] = back_ref[...]
    add_products(total_in, total_out, grad_ref, [(chunk_ref, pl.multiple_of(plan_ref[place] * 2 * half, 2 * half))])


def last(plan, total, front, back, place, held_grad):
    half, rows = front.shape
    return call(
        functools.partial(last_body, place),
        "last",
        [plan],
        [(total, True), (held_grad, True), (front, True), (back, True)],
        [(total.shape, jnp.float32, True)],
        [pltpu.VMEM((2 * half, rows), front.dtype)],
        {0: 0},
        flops=4 * half * total.size,
        traffic=8 * total.size,
    )[0]


def pack_body(ids_ref, total_ref, *refs):
    packed_ref, rows_ref = refs[-2:]
    if packed_ref.dtype == jnp.float32:
        gather_rows(look_in(ids_ref), packed_ref.shape[0], [(total_ref, packed_ref)])
    else:
        gather_rows(look_in(ids_ref), packed_ref.shape[0], [(total_ref, rows_ref)])
        packed_ref[...] = rows_ref[...].astype(packed_ref.dtype)


def pack(ids, total, place, kind, after=()):
    shape = (ids.shape[2] - LANES, LANES)
    return call(
        pack_body,
        "pack",
        [],
        [ids_of(ids, place), (total, True)] + [(v, True) for v in after],
        [(shape, kind, True)],
        [pltpu.VMEM(shape, jnp.float32)],
        traffic=40 * shape[0] * LANES,
    )[0]


def clear(ids_ref, total_ref):
    zero = jnp.zeros((1, LANES), jnp.float32)

    def body(rows):
        for at in [ids_ref[0, i] for i in rows]:
            total_ref[pl.ds(at, 1), :] = zero

    each_group(ids_ref.shape[1] - LANES, body)


def close_body(others, own_ids, *refs):
    total_ref, packed_ref = refs[-2:]
    gather_rows(look_in(own_ids), packed_ref.shape[0], [(total_ref, packed_ref)])
    for ids_ref in (own_ids, *refs[:others]):
        clear(ids_ref, total_ref)


def close(ids, total, place, others, after):
    return call(
        functools.partial(close_body, len(others)),
        "close",
        [],
        [ids_of(ids, p) for p in (place, *others)] + [(total, True)] + [(v, True) for v in after],
        [(total.shape, jnp.float32, True), ((ids.shape[2] - LANES, LANES), jnp.float32, True)],
        (),
        {1 + len(others): 0},
        traffic=WEIGHT * total.size,
    )


def spread_one(ids_ref, update_ref, wide_ref, out_ref, rows_ref, block_ref, sems, first):
    per_owner, count = block_ref.shape[0], update_ref.shape[0]
    at = pl.ds(pl.multiple_of(ids_ref[0, count] * per_owner, 2 * SUBLANES), per_owner)
    rows_ref[...] = update_ref[...].astype(jnp.float32)
    scatter_rows(look_in(ids_ref), count, [(rows_ref, wide_ref)])
    block_ref[...] = wide_ref[at, :].astype(block_ref.dtype)
    copies = split_copies(block_ref, out_ref.at[at], 2, sems, first)
    start_all(copies)
    return copies


def store_body(dp_count, ids_ref, total_ref, *refs):
    refs = refs[3:]
    new, update_ref, refs = refs[:3], refs[4], refs[5:]
    helds, wide_ref, residual_ref, outs, out_ref = refs[:3], refs[3], refs[4], refs[5:8], refs[8]
    rows_ref, block_ref, sems = refs[9:]
    per_owner, count = block_ref.shape[0], update_ref.shape[0]
    copies = []
    used = 0

    def begin(source, target, parts):
        nonlocal used
        copies.extend(split_copies(source, target, parts, sems, used))
        start_all(copies[-parts:])
        used += parts

    begin(total_ref, residual_ref, 2 * dp_count)
    begin_at = look_from(ids_ref, per_owner, count)
    for n in range(3):
        scatter_rows(begin_at, count, [(new[n], helds[n])])
        begin(helds[n], outs[n], 2)
    copies.extend(spread_one(ids_ref, update_ref, wide_ref, out_ref, rows_ref, block_ref, sems, used))
    wait_all(copies)


def store(ids, total, helds, updates, wide, rounded, place):
    size, count, dp_count = helds[0].shape, ids.shape[2] - LANES, ids.shape[0]
    out = call(
        functools.partial(store_body, dp_count),
        "store",
        [],
        [ids_of(ids, place)] + [(v, True) for v in [total, *helds, *updates, wide, rounded]],
        [(size, jnp.float32, True)] * 3
        + [(wide.shape, jnp.float32, True), (total.shape, jnp.float32, False)]
        + [(size, jnp.float32, False)] * 3
        + [(wide.shape, rounded.dtype, False)],
        [pltpu.VMEM((count, LANES), jnp.float32), pltpu.VMEM(size, rounded.dtype), DMA((8 + 2 * dp_count,))],
        {2: 0, 3: 1, 4: 2, 8: 3},
        traffic=4 * WEIGHT * size[0] * LANES,
    )
    return out[4], out[5:8], out[3], out[8]


def relay(values, after):
    return call(
        lambda *_: None,
        "relay",
        [],
        [(values, True), (away(after), False)],
        [(values.shape, values.dtype, True)],
        (),
        {0: 0},
    )[0]


def spread_body(count, *refs):
    ids, updates = refs[:count], refs[count + 1 : 2 * count + 1]
    wide_ref, out_ref, rows_ref, blocks_ref, sems = refs[2 * count + 2 :]
    copies = []
    for n in range(count):
        copies += spread_one(ids[n], updates[n], wide_ref, out_ref, rows_ref, blocks_ref.at[n], sems, 2 * n)
    wait_all(copies)


def spread(ids, wide, earlier, updates, places):
    dp_count, n = ids.shape[0], len(places)
    kind = updates[0].dtype
    return call(
        functools.partial(spread_body, n),
        "spread",
        [],
        [ids_of(ids, place) for place in places] + [(wide, True)] + [(v, True) for v in updates] + [(earlier, False)],
        [(wide.shape, jnp.float32, True), (wide.shape, kind, False)],
        [
            pltpu.VMEM(updates[0].shape, jnp.float32),
            pltpu.VMEM((n, wide.shape[0] // dp_count, LANES), kind),
            DMA((2 * n,)),
        ],
        {n: 0, 1 + 2 * n: 1},
        traffic=WEIGHT * wide.size,
    )


def local(table, ring, activations, out_grad, residual, chosen, master, moment_one, moment_two, params):
    token_grad = out_grad[0]
    own = activations[0]
    tokens, row_count = own.shape
    column_count = token_grad.shape[1]
    dp_count, tensor_count = table.shape[:2]
    chips = dp_count // 2
    owner_rows = row_count // dp_count

    plan = jnp.asarray(table)[lax.axis_index("dp"), lax.axis_index("tensor")]
    ahead = [(ring[i], ring[(i + 1) % tensor_count]) for i in range(tensor_count)]
    behind = [(b, a) for a, b in ahead]

    def place_of(k, j):
        return 2 * k + j

    def swap(values):
        return lax.ppermute(values, "dp", [(d, d ^ 1) for d in range(dp_count)])

    def send(values, k):
        return lax.ppermute(values, "dp", [(d, ((d // 2 + k) % chips) * 2 + d % 2) for d in range(dp_count)])

    own_place = place_of(0, 0)
    states = [tiles(v) for v in (moment_one, moment_two, master)]
    front, back = lax.ppermute(own, "tensor", ahead), lax.ppermute(own, "tensor", behind)
    def chunks_of(hop):
        return [tensor_count - hop, hop] if hop < tensor_count // 2 else [hop]

    total, held_grad, ids = load(plan, residual[0], token_grad, own, chosen, chunks_of(1))
    for hop in range(1, tensor_count // 2):
        chunks = [front, back]
        if hop == tensor_count // 2 - 1:
            front, back = front[: tokens // 2], back[tokens // 2 :]
        front, back = lax.ppermute(front, "tensor", ahead), lax.ppermute(back, "tensor", behind)
        side, sources = None, ()
        if hop == tensor_count // 2 - 1:
            side, sources = "pick", [*helds, ids_of(ids, own_place)]
        elif hop == 1:
            side, sources = "states", states
        elif hop == 2:
            side, sources = "params", [tiles(params)]
        total, held_grad, *fetched = accumulate(
            plan, total, chunks, chunks_of(hop), held_grad, token_grad, chunks_of(hop + 1), side, sources
        )
        if side == "states":
            helds = fetched
        if side == "params":
            (wide,) = fetched
        if side == "pick":
            picked = fetched
    total = tiles(last(plan, total, front, back, tensor_count // 2, held_grad))

    received, sums = [], []
    for k in range(1, chips):
        other = swap(pack(ids, total, place_of(k, 1), jnp.bfloat16))
        mine = pack(ids, total, place_of(k, 0), jnp.float32)
        sums.append((mine + other.astype(jnp.float32)).astype(jnp.bfloat16))
        received.append(send(sums[-1], k))
    other = pack(ids, total, place_of(0, 1), jnp.bfloat16, sums)
    received.append(swap(other))
    total, mine = close(ids, total, own_place, range(1, dp_count), [*sums, other])
    for part in received:
        mine = mine + part.astype(jnp.float32)
    mean_grad = mine / dp_count

    one, two, weights = picked
    one = beta_one * one + (1.0 - beta_one) * mean_grad
    two = beta_two * two + (1.0 - beta_two) * mean_grad * mean_grad
    weights = weights - learn_rate * (one / (jnp.sqrt(two) + epsilon) + decay_rate * weights)
    rounded = weights.astype(jnp.bfloat16)

    far = [send(rounded, k) for k in range(1, chips)]
    near = swap(rounded)
    new_residual, fresh, wide, out = store(
        ids, total, helds, [one, two, weights], wide, rounded, own_place
    )
    for k in range(1, chips):
        direct = relay(far[k - 1], out)
        across = swap(direct)
        updates, places = [direct], [place_of(chips - k, 0)]
        if k == 1:
            updates, places = [near, *updates], [place_of(0, 1), *places]
        wide, out = spread(ids, wide, out, updates, places)
        wide, out = spread(ids, wide, out, [across], [place_of(chips - k, 1)])

    new_one, new_two, new_master = (untiles(v, owner_rows, column_count) for v in fresh)
    return (
        untiles(new_residual, row_count, column_count)[None],
        new_one,
        new_two,
        new_master,
        untiles(out, row_count, column_count),
    )


def solution(mesh):
    dp_count, tensor_count = mesh.shape["dp"], mesh.shape["tensor"]
    body = functools.partial(local, plan_table(dp_count, tensor_count), ring_order(tensor_count))
    in_specs = (
        P("dp", "tensor", None),
        P("dp", None, "tensor"),
        P("dp", None, "tensor"),
        P(None, "tensor", None),
        P("dp", "tensor"),
        P("dp", "tensor"),
        P("dp", "tensor"),
        P(None, "tensor"),
    )
    out_specs = (
        P("dp", None, "tensor"),
        P("dp", "tensor"),
        P("dp", "tensor"),
        P("dp", "tensor"),
        P(None, "tensor"),
    )
    return jax.shard_map(body, mesh=mesh, in_specs=in_specs, out_specs=out_specs, check_vma=False)
```

```python
import functools
import jax
import jax.numpy as jnp
import numpy as np
from jax import lax
from jax.experimental import pallas as pl
from jax.experimental.pallas import tpu as pltpu
from jax.sharding import PartitionSpec as P

beta_one = 0.9
beta_two = 0.999
learn_rate = 0.01
decay_rate = 0.1
epsilon = 1e-08
LANES = 128
SUBLANES = 8
UNROLL = 32


def ring_order(count):
    inner = 4 if count % 16 == 0 else 2
    outer = count // inner
    cells = []
    for row in range(outer):
        steps = range(1, inner) if row % 2 == 0 else range(inner - 1, 0, -1)
        cells += [row * inner + step for step in steps]
    return cells + [row * inner for row in range(outer - 1, -1, -1)]


def plan_table(dp_count, tensor_count):
    ring = ring_order(tensor_count)
    place = {cell: i for i, cell in enumerate(ring)}
    chips = dp_count // 2
    table = np.zeros((dp_count, tensor_count, tensor_count + dp_count), np.int32)
    for d in range(dp_count):
        owners = [((d // 2 + k) % chips) * 2 + ((d % 2) ^ j) for k in range(chips) for j in range(2)]
        for t in range(tensor_count):
            table[d, t, :tensor_count] = [ring[(place[t] + j) % tensor_count] for j in range(tensor_count)]
            table[d, t, tensor_count:] = owners
    return table


def tiles(values):
    rows, columns = values.shape
    split = values.reshape(rows // SUBLANES, SUBLANES, columns // LANES, LANES)
    return split.transpose(0, 2, 1, 3).reshape(rows * columns // LANES, LANES)


def untiles(values, rows, columns):
    split = values.reshape(rows // SUBLANES, columns // LANES, SUBLANES, LANES)
    return split.transpose(0, 2, 1, 3).reshape(rows, columns)


VMEM = pltpu.MemorySpace.VMEM
HELD = pl.BlockSpec(memory_space=VMEM)
AWAY = pl.BlockSpec(memory_space=pl.ANY)
DMA = pltpu.SemaphoreType.DMA
WIDTH = 1792
WEIGHT = 24
PARTS = 4


def each_group(count, body):
    def step(i, carry):
        body([i * UNROLL + k for k in range(UNROLL)])
        return carry

    lax.fori_loop(0, count // UNROLL, step, 0)


def gather_rows(look, count, pairs):
    def move(rows):
        at = [look(i) for i in rows]
        for source, target in pairs:
            values = [source[pl.ds(a, 1), :] for a in at]
            for i, value in zip(rows, values):
                target[pl.ds(i, 1), :] = value

    each_group(count, move)


def scatter_rows(look, count, pairs):
    def move(rows):
        at = [look(i) for i in rows]
        for source, target in pairs:
            values = [source[pl.ds(i, 1), :] for i in rows]
            for a, value in zip(at, values):
                target[pl.ds(a, 1), :] = value

    each_group(count, move)


def product(a, b):
    return lax.dot_general(a, b, (((0,), (0,)), ((), ())), preferred_element_type=jnp.float32)


def add_products(total_in, total_out, grad_ref, terms, beside=None):
    columns = grad_ref.shape[1]
    width = WIDTH if columns % WIDTH == 0 else LANES

    def step(i, carry):
        at = pl.ds(pl.multiple_of(i * width, LANES), width)
        total = total_in[:, at]
        for chunk, start in terms:
            total = total + product(chunk[...], grad_ref[pl.ds(start, chunk.shape[0]), at])
        total_out[:, at] = total
        if beside is not None:
            beside(i, columns // width)
        return carry

    lax.fori_loop(0, columns // width, step, 0)


def split_copies(source, target, parts, sems, first=0):
    size = source.shape[0] // parts
    return [
        pltpu.make_async_copy(source.at[pl.ds(k * size, size)], target.at[pl.ds(k * size, size)], sems.at[first + k])
        for k in range(parts)
    ]


def start_all(copies):
    for copy in copies:
        copy.start()


def wait_all(copies):
    for copy in copies:
        copy.wait()


def away(values):
    return pltpu.with_memory_space_constraint(values, pltpu.MemorySpace.HBM)


def call(body, name, scalars, operands, outs, scratch=(), aliases=None, flops=0, traffic=0):
    return pl.pallas_call(
        body,
        out_shape=[
            pltpu.VMEM(shape, kind) if held else jax.ShapeDtypeStruct(shape, kind) for shape, kind, held in outs
        ],
        grid_spec=pltpu.PrefetchScalarGridSpec(
            num_scalar_prefetch=len(scalars),
            grid=(1,),
            in_specs=[held if isinstance(held, pl.BlockSpec) else HELD if held else AWAY for _, held in operands],
            out_specs=[HELD if held else AWAY for _, _, held in outs],
            scratch_shapes=list(scratch),
        ),
        input_output_aliases={len(scalars) + k: v for k, v in (aliases or {}).items()},
        cost_estimate=pl.CostEstimate(flops=flops, bytes_accessed=traffic, transcendentals=0),
        compiler_params=pltpu.CompilerParams(vmem_limit_bytes=14 << 20),
        name=name,
    )(*scalars, *(values for values, _ in operands))


def look_in(ids_ref):
    return lambda i: ids_ref[0, i]


def ids_of(ids, place):
    return ids, pl.BlockSpec((None, *ids.shape[1:]), lambda i, *_: (place, 0, 0), memory_space=pltpu.SMEM)


def order_ids(plan_ref, spans_ref, ids_ref, own_ids_ref, columns, rows):
    dp_count, _, count = spans_ref.shape
    blocks = columns // LANES
    per_owner = rows // dp_count * blocks
    factor = -(-(1 << 18) // blocks)
    assert per_owner * (factor * blocks - (1 << 18)) < 1 << 18
    for p in range(dp_count):
        owner = plan_ref[plan_ref.shape[0] - dp_count + p]
        spans = spans_ref[owner]
        row = lax.shift_right_logical(spans * factor, 18)
        column = spans - row * blocks
        tile = lax.shift_right_logical(row, 3) * blocks + column
        place = tile * SUBLANES + (row & 7)
        ids_ref[p, :, :count] = place + owner * per_owner
        if p == 0:
            own_ids_ref[0] = place
        ids_ref[p, :, count:] = jnp.full((1, LANES), 1, jnp.int32) * owner


def slot_of(place, tensor_count):
    if place in (0, tensor_count // 2):
        return 0 if place == 0 else tensor_count - 1
    return 2 * place if place < tensor_count // 2 else 2 * (tensor_count - place) - 1


def grad_copies(plan_ref, places, tokens, grad_ref, held_ref, sems, first=0):
    half, copies = tokens // 2, []
    for n, j in enumerate(places):
        slot = slot_of(j, held_ref.shape[0] // tokens)
        for k in range(2):
            at = pl.ds(pl.multiple_of(plan_ref[j] * tokens + k * half, half), half)
            to = pl.ds(slot * tokens + k * half, half)
            copies.append(pltpu.make_async_copy(grad_ref.at[at], held_ref.at[to], sems.at[first + 2 * n + k]))
    return copies


def load_body(places, plan_ref, residual_ref, grad_ref, own_ref, spans_ref, *refs):
    total_ref, held_ref, own_held, ids_ref, own_ids_ref, spans_held, sems, own_sems = refs
    tokens = own_ref.shape[0]
    spans_copy = pltpu.make_async_copy(spans_ref, spans_held, own_sems.at[1])
    spans_copy.start()
    copies = [pltpu.make_async_copy(own_ref, own_held, own_sems.at[0])]
    copies += split_copies(residual_ref, total_ref, 8, sems)
    copies += grad_copies(plan_ref, places, tokens, grad_ref, held_ref, sems, 8)
    start_all(copies)
    spans_copy.wait()
    order_ids(plan_ref, spans_held, ids_ref, own_ids_ref, total_ref.shape[1], total_ref.shape[0])
    wait_all(copies)


def load(plan, residual, token_grad, own, spans, places):
    dp_count, _, count = spans.shape
    return call(
        functools.partial(load_body, places),
        "load",
        [plan],
        [(away(residual), False), (away(token_grad), False), (away(own), False), (away(spans), False)],
        [
            (residual.shape, jnp.float32, True),
            (token_grad.shape, token_grad.dtype, True),
            (own.shape, own.dtype, True),
            ((dp_count, 1, count + LANES), jnp.int32, True),
            ((1, 1, count), jnp.int32, True),
        ],
        [pltpu.VMEM(spans.shape, jnp.int32), DMA((8 + 2 * len(places),)), DMA((2,))],
        flops=WEIGHT * own.size * residual.shape[1],
        traffic=WEIGHT * residual.size,
    )


def accumulate_body(places, coming, tokens, side, plan_ref, total_in, held_in, grad_ref, *refs):
    chunks, refs = refs[: len(places)], refs[len(places) :]
    starts = [slot_of(j, held_in.shape[0] // tokens) * tokens for j in places]
    extra = {"states": 3, "params": 1, "pick": 4}.get(side, 0)
    sources, (total_out, held_ref), refs = refs[:extra], refs[extra : extra + 2], refs[extra + 2 :]
    sems = refs[-1]
    copies = grad_copies(plan_ref, coming, tokens, grad_ref, held_ref, sems, 6)
    if side == "states":
        helds = refs[:3]
        copies += [c for n in range(3) for c in split_copies(sources[n], helds[n], 2, sems, 2 * n)]
    if side == "params":
        wide_ref, narrow_ref = refs[:2]
        copies += split_copies(sources[0], narrow_ref, 4, sems)
    start_all(copies)
    beside = None
    if side == "pick":

        def beside(i, steps):
            share = refs[0].shape[0] // steps
            for first in range(0, share, UNROLL):
                rows = [i * share + first + k for k in range(UNROLL)]
                at = [sources[3][0, row] for row in rows]
                for source, target in zip(sources[:3], refs[:3]):
                    values = [source[pl.ds(a, 1), :] for a in at]
                    for row, value in zip(rows, values):
                        target[pl.ds(row, 1), :] = value

    add_products(total_in, total_out, held_ref, list(zip(chunks, starts)), beside)
    wait_all(copies)
    if side == "params":
        wide_ref[...] = narrow_ref[...].astype(jnp.float32)


def accumulate(plan, total, chunks, places, held_grad, token_grad, coming, side=None, sources=()):
    tokens = chunks[0].shape[0]
    outs, scratch = [(total.shape, jnp.float32, True), (held_grad.shape, held_grad.dtype, True)], []
    inputs = []
    if side == "states":
        inputs = [(away(v), False) for v in sources]
        outs += [(sources[0].shape, jnp.float32, True)] * 3
    if side == "pick":
        count = sources[3][0].shape[2]
        inputs = [(v, True) for v in sources[:3]] + [sources[3]]
        outs += [((count, LANES), jnp.float32, True)] * 3
    if side == "params":
        inputs = [(away(sources[0]), False)]
        outs += [(sources[0].shape, jnp.float32, True)]
        scratch = [pltpu.VMEM(sources[0].shape, sources[0].dtype)]
    return call(
        functools.partial(accumulate_body, places, coming, tokens, side),
        "accumulate",
        [plan],
        [(total, True), (held_grad, True), (away(token_grad), False)] + [(c, True) for c in chunks] + inputs,
        outs,
        scratch + [DMA((6 + 2 * len(coming),))],
        {0: 0, 1: 1},
        flops=WEIGHT * tokens * total.size * len(chunks),
        traffic=WEIGHT * total.size,
    )


def last_body(total_in, grad_ref, front_ref, back_ref, total_out, chunk_ref):
    half = front_ref.shape[0]
    chunk_ref[:half] = front_ref[...]
    chunk_ref[half:] = back_ref[...]
    add_products(total_in, total_out, grad_ref, [(chunk_ref, grad_ref.shape[0] - 2 * half)])


def last(total, front, back, held_grad):
    half, rows = front.shape
    return call(
        last_body,
        "last",
        [],
        [(total, True), (held_grad, True), (front, True), (back, True)],
        [(total.shape, jnp.float32, True)],
        [pltpu.VMEM((2 * half, rows), front.dtype)],
        {0: 0},
        flops=4 * half * total.size,
        traffic=8 * total.size,
    )[0]


def pack_body(ids_ref, total_ref, *refs):
    packed_ref, rows_ref = refs[-2:]
    if packed_ref.dtype == jnp.float32:
        gather_rows(look_in(ids_ref), packed_ref.shape[0], [(total_ref, packed_ref)])
    else:
        gather_rows(look_in(ids_ref), packed_ref.shape[0], [(total_ref, rows_ref)])
        packed_ref[...] = rows_ref[...].astype(packed_ref.dtype)


def pack(ids, total, place, kind, after=()):
    shape = (ids.shape[2] - LANES, LANES)
    return call(
        pack_body,
        "pack",
        [],
        [ids_of(ids, place), (total, True)] + [(v, True) for v in after],
        [(shape, kind, True)],
        [pltpu.VMEM(shape, jnp.float32)],
        traffic=40 * shape[0] * LANES,
    )[0]


def clear(ids_ref, total_ref):
    zero = jnp.zeros((1, LANES), jnp.float32)

    def body(rows):
        for at in [ids_ref[0, i] for i in rows]:
            total_ref[pl.ds(at, 1), :] = zero

    each_group(ids_ref.shape[1] - LANES, body)


def close_body(others, own_ids, *refs):
    total_ref, packed_ref = refs[-2:]
    gather_rows(look_in(own_ids), packed_ref.shape[0], [(total_ref, packed_ref)])
    for ids_ref in (own_ids, *refs[:others]):
        clear(ids_ref, total_ref)


def close(ids, total, place, others, after):
    return call(
        functools.partial(close_body, len(others)),
        "close",
        [],
        [ids_of(ids, p) for p in (place, *others)] + [(total, True)] + [(v, True) for v in after],
        [(total.shape, jnp.float32, True), ((ids.shape[2] - LANES, LANES), jnp.float32, True)],
        (),
        {1 + len(others): 0},
        traffic=total.size // 4,
    )


def spread_one(ids_ref, update_ref, wide_ref, out_ref, rows_ref, block_ref, sems, first):
    per_owner, count = block_ref.shape[0], update_ref.shape[0]
    at = pl.ds(pl.multiple_of(ids_ref[0, count] * per_owner, 2 * SUBLANES), per_owner)
    rows_ref[...] = update_ref[...].astype(jnp.float32)
    scatter_rows(look_in(ids_ref), count, [(rows_ref, wide_ref)])
    return narrow(wide_ref.at[at], block_ref, out_ref.at[at], sems, first)


def narrow(source, block_ref, target, sems, first):
    copies = split_copies(block_ref, target, PARTS, sems, first)
    size = block_ref.shape[0] // PARTS
    for k, copy in enumerate(copies):
        block_ref[k * size : (k + 1) * size, :] = source[k * size : (k + 1) * size, :].astype(block_ref.dtype)
        copy.start()
    return copies


def store_body(dp_count, own_ids_ref, *refs):
    ids, total_in, refs = refs[:dp_count], refs[dp_count], refs[dp_count + 1 + 3 :]
    new, update_ref, refs = refs[:3], refs[4], refs[5:]
    total_ref, helds, wide_ref, residual_ref, outs, out_ref = refs[0], refs[1:4], refs[4], refs[5], refs[6:9], refs[9]
    rows_ref, block_ref, sems = refs[10:]
    per_owner, count = block_ref.shape[0], update_ref.shape[0]
    copies = []

    def begin(source, target):
        copies.extend(split_copies(source, target, 2, sems, len(copies)))
        start_all(copies[-2:])

    def block(p):
        return pl.ds(pl.multiple_of(ids[p][0, count] * per_owner, 2 * SUBLANES), per_owner)

    def flush(p):
        begin(total_ref.at[block(p)], residual_ref.at[block(p)])

    for p in (0, *range(2, dp_count)):
        flush(p)
    clear(ids[1], total_ref)
    flush(1)
    rows_ref[...] = update_ref[...].astype(jnp.float32)
    pairs = [*zip(new, helds), (rows_ref, wide_ref.at[block(0)])]
    scatter_rows(look_in(own_ids_ref), count, pairs)
    for held, out in zip(helds, outs):
        begin(held, out)
    copies += narrow(wide_ref.at[block(0)], block_ref, out_ref.at[block(0)], sems, len(copies))
    wait_all(copies)


def store(ids, own_ids, total, helds, updates, wide, rounded):
    size, count, dp_count = helds[0].shape, own_ids.shape[2], ids.shape[0]
    n = dp_count + 1
    out = call(
        functools.partial(store_body, dp_count),
        "store",
        [],
        [ids_of(own_ids, 0)]
        + [ids_of(ids, p) for p in range(dp_count)]
        + [(v, True) for v in [total, *helds, *updates, wide, rounded]],
        [(total.shape, jnp.float32, True)]
        + [(size, jnp.float32, True)] * 3
        + [(wide.shape, jnp.float32, True), (total.shape, jnp.float32, False)]
        + [(size, jnp.float32, False)] * 3
        + [(wide.shape, rounded.dtype, False)],
        [pltpu.VMEM((count, LANES), jnp.float32), pltpu.VMEM(size, rounded.dtype), DMA((6 + PARTS + 2 * dp_count,))],
        {n: 0, n + 1: 1, n + 2: 2, n + 3: 3, n + 7: 4},
        traffic=4 * WEIGHT * size[0] * LANES,
    )
    return out[5], out[6:9], out[4], out[9]


def relay(values, after):
    return call(
        lambda *_: None,
        "relay",
        [],
        [(values, True), after],
        [(values.shape, values.dtype, True)],
        (),
        {0: 0},
    )[0]


def spread_body(count, *refs):
    ids, updates = refs[:count], refs[count + 1 : 2 * count + 1]
    wide_ref, out_ref, rows_ref, blocks_ref, sems = refs[2 * count + 2 :]
    copies = []
    for n in range(count):
        copies += spread_one(ids[n], updates[n], wide_ref, out_ref, rows_ref, blocks_ref.at[n], sems, PARTS * n)
    wait_all(copies)


def spread(ids, wide, earlier, updates, places):
    dp_count, n = ids.shape[0], len(places)
    kind = updates[0].dtype
    return call(
        functools.partial(spread_body, n),
        "spread",
        [],
        [ids_of(ids, place) for place in places] + [(wide, True)] + [(v, True) for v in updates] + [(earlier, False)],
        [(wide.shape, jnp.float32, True), (wide.shape, kind, False)],
        [
            pltpu.VMEM(updates[0].shape, jnp.float32),
            pltpu.VMEM((n, wide.shape[0] // dp_count, LANES), kind),
            DMA((PARTS * n,)),
        ],
        {n: 0, 1 + 2 * n: 1},
        traffic=WEIGHT * wide.size,
    )


def local(table, ring, activations, out_grad, residual, chosen, master, moment_one, moment_two, params):
    token_grad = out_grad[0]
    own = activations[0]
    tokens, row_count = own.shape
    column_count = token_grad.shape[1]
    dp_count, tensor_count = table.shape[:2]
    chips = dp_count // 2
    owner_rows = row_count // dp_count

    plan = jnp.asarray(table)[lax.axis_index("dp"), lax.axis_index("tensor")]
    ahead = [(ring[i], ring[(i + 1) % tensor_count]) for i in range(tensor_count)]
    behind = [(b, a) for a, b in ahead]

    def place_of(k, j):
        return 2 * k + j

    def swap(values):
        return lax.ppermute(values, "dp", [(d, d ^ 1) for d in range(dp_count)])

    def send(values, k):
        return lax.ppermute(values, "dp", [(d, ((d // 2 + k) % chips) * 2 + d % 2) for d in range(dp_count)])

    own_place = place_of(0, 0)
    states = [tiles(v) for v in (moment_one, moment_two, master)]
    front, back = lax.ppermute(own, "tensor", ahead), lax.ppermute(own, "tensor", behind)
    def chunks_of(hop):
        return [tensor_count - hop, hop] if hop < tensor_count // 2 else [hop]

    total, held_grad, own, ids, own_ids = load(plan, residual[0], token_grad, own, chosen, [0, *chunks_of(1)])
    for hop in range(1, tensor_count // 2):
        chunks, places = [front, back], chunks_of(hop)
        if hop == 1:
            chunks, places = [own, *chunks], [0, *places]
        if hop == tensor_count // 2 - 1:
            front, back = front[: tokens // 2], back[tokens // 2 :]
        front, back = lax.ppermute(front, "tensor", ahead), lax.ppermute(back, "tensor", behind)
        side, sources = None, ()
        if hop == tensor_count // 2 - 1:
            side, sources = "pick", [*helds, ids_of(own_ids, 0)]
        elif hop == 1:
            side, sources = "states", states
        elif hop == 2:
            side, sources = "params", [tiles(params)]
        total, held_grad, *fetched = accumulate(
            plan, total, chunks, places, held_grad, token_grad, chunks_of(hop + 1), side, sources
        )
        if side == "states":
            helds = fetched
        if side == "params":
            (wide,) = fetched
        if side == "pick":
            picked = fetched
    total = tiles(last(total, front, back, held_grad))

    received, sums = [], []
    for k in range(1, chips):
        other = swap(pack(ids, total, place_of(k, 1), jnp.bfloat16))
        mine = pack(ids, total, place_of(k, 0), jnp.float32)
        sums.append((mine + other.astype(jnp.float32)).astype(jnp.bfloat16))
        received.append(send(sums[-1], k))
    other = pack(ids, total, place_of(0, 1), jnp.bfloat16, sums)
    received.append(swap(other))
    total, mine = close(ids, total, own_place, range(2, dp_count), [*sums, other])
    received[0] = relay(received[0], (mine, True))
    for part in received:
        mine = mine + part.astype(jnp.float32)
    mean_grad = mine / dp_count

    one, two, weights = picked
    one = beta_one * one + (1.0 - beta_one) * mean_grad
    two = beta_two * two + (1.0 - beta_two) * mean_grad * mean_grad
    weights = weights - learn_rate * (one / (jnp.sqrt(two) + epsilon) + decay_rate * weights)
    rounded = weights.astype(jnp.bfloat16)

    far = [send(rounded, k) for k in range(1, chips)]
    near = swap(rounded)
    new_residual, fresh, wide, out = store(
        ids, own_ids, total, helds, [one, two, weights], wide, rounded
    )
    for k in range(1, chips):
        direct = relay(far[k - 1], (away(out), False))
        across = swap(direct)
        updates, places = [direct], [place_of(chips - k, 0)]
        if k == 1:
            updates, places = [near, *updates], [place_of(0, 1), *places]
        wide, out = spread(ids, wide, out, updates, places)
        wide, out = spread(ids, wide, out, [across], [place_of(chips - k, 1)])

    new_one, new_two, new_master = (untiles(v, owner_rows, column_count) for v in fresh)
    return (
        untiles(new_residual, row_count, column_count)[None],
        new_one,
        new_two,
        new_master,
        untiles(out, row_count, column_count),
    )


def solution(mesh):
    dp_count, tensor_count = mesh.shape["dp"], mesh.shape["tensor"]
    body = functools.partial(local, plan_table(dp_count, tensor_count), ring_order(tensor_count))
    in_specs = (
        P("dp", "tensor", None),
        P("dp", None, "tensor"),
        P("dp", None, "tensor"),
        P(None, "tensor", None),
        P("dp", "tensor"),
        P("dp", "tensor"),
        P("dp", "tensor"),
        P(None, "tensor"),
    )
    out_specs = (
        P("dp", None, "tensor"),
        P("dp", "tensor"),
        P("dp", "tensor"),
        P("dp", "tensor"),
        P(None, "tensor"),
    )
    return jax.shard_map(body, mesh=mesh, in_specs=in_specs, out_specs=out_specs, check_vma=False)
```

```python
import functools
import jax
import jax.numpy as jnp
import numpy as np
from jax import lax
from jax.experimental import pallas as pl
from jax.experimental.pallas import tpu as pltpu
from jax.sharding import PartitionSpec as P

beta_one = 0.9
beta_two = 0.999
learn_rate = 0.01
decay_rate = 0.1
epsilon = 1e-08
LANES = 128
SUBLANES = 8
UNROLL = 32


def ring_order(count):
    inner = 4 if count % 16 == 0 else 2
    outer = count // inner
    cells = []
    for row in range(outer):
        steps = range(1, inner) if row % 2 == 0 else range(inner - 1, 0, -1)
        cells += [row * inner + step for step in steps]
    return cells + [row * inner for row in range(outer - 1, -1, -1)]


def plan_table(dp_count, tensor_count):
    ring = ring_order(tensor_count)
    place = {cell: i for i, cell in enumerate(ring)}
    chips = dp_count // 2
    table = np.zeros((dp_count, tensor_count, tensor_count + dp_count), np.int32)
    for d in range(dp_count):
        owners = [((d // 2 + k) % chips) * 2 + ((d % 2) ^ j) for k in range(chips) for j in range(2)]
        for t in range(tensor_count):
            table[d, t, :tensor_count] = [ring[(place[t] + j) % tensor_count] for j in range(tensor_count)]
            table[d, t, tensor_count:] = owners
    return table


def tiles(values):
    rows, columns = values.shape
    split = values.reshape(rows // SUBLANES, SUBLANES, columns // LANES, LANES)
    return split.transpose(0, 2, 1, 3).reshape(rows * columns // LANES, LANES)


def untiles(values, rows, columns):
    split = values.reshape(rows // SUBLANES, columns // LANES, SUBLANES, LANES)
    return split.transpose(0, 2, 1, 3).reshape(rows, columns)


VMEM = pltpu.MemorySpace.VMEM
HELD = pl.BlockSpec(memory_space=VMEM)
AWAY = pl.BlockSpec(memory_space=pl.ANY)
DMA = pltpu.SemaphoreType.DMA
WIDTH = 1792
WEIGHT = 24
PARTS = 4


def each_group(count, body):
    def step(i, carry):
        body([i * UNROLL + k for k in range(UNROLL)])
        return carry

    lax.fori_loop(0, count // UNROLL, step, 0)


def gather_rows(look, count, pairs):
    def move(rows):
        at = [look(i) for i in rows]
        for source, target in pairs:
            values = [source[pl.ds(a, 1), :] for a in at]
            for i, value in zip(rows, values):
                target[pl.ds(i, 1), :] = value

    each_group(count, move)


def scatter_rows(look, count, pairs):
    def move(rows):
        at = [look(i) for i in rows]
        for source, target in pairs:
            values = [source[pl.ds(i, 1), :] for i in rows]
            for a, value in zip(at, values):
                target[pl.ds(a, 1), :] = value

    each_group(count, move)


def product(a, b):
    return lax.dot_general(a, b, (((0,), (0,)), ((), ())), preferred_element_type=jnp.float32)


def add_products(total_in, total_out, grad_ref, terms, beside=None):
    columns = grad_ref.shape[1]
    width = WIDTH if columns % WIDTH == 0 else LANES

    def step(i, carry):
        at = pl.ds(pl.multiple_of(i * width, LANES), width)
        total = total_in[:, at]
        for chunk, start in terms:
            total = total + product(chunk[...], grad_ref[pl.ds(start, chunk.shape[0]), at])
        total_out[:, at] = total
        if beside is not None:
            beside(i, columns // width)
        return carry

    lax.fori_loop(0, columns // width, step, 0)


def split_copies(source, target, parts, sems, first=0):
    size = source.shape[0] // parts
    return [
        pltpu.make_async_copy(source.at[pl.ds(k * size, size)], target.at[pl.ds(k * size, size)], sems.at[first + k])
        for k in range(parts)
    ]


def start_all(copies):
    for copy in copies:
        copy.start()


def wait_all(copies):
    for copy in copies:
        copy.wait()


def away(values):
    return pltpu.with_memory_space_constraint(values, pltpu.MemorySpace.HBM)


def call(body, name, scalars, operands, outs, scratch=(), aliases=None, flops=0, traffic=0):
    return pl.pallas_call(
        body,
        out_shape=[
            pltpu.VMEM(shape, kind) if held else jax.ShapeDtypeStruct(shape, kind) for shape, kind, held in outs
        ],
        grid_spec=pltpu.PrefetchScalarGridSpec(
            num_scalar_prefetch=len(scalars),
            grid=(1,),
            in_specs=[held if isinstance(held, pl.BlockSpec) else HELD if held else AWAY for _, held in operands],
            out_specs=[HELD if held else AWAY for _, _, held in outs],
            scratch_shapes=list(scratch),
        ),
        input_output_aliases={len(scalars) + k: v for k, v in (aliases or {}).items()},
        cost_estimate=pl.CostEstimate(flops=flops, bytes_accessed=traffic, transcendentals=0),
        compiler_params=pltpu.CompilerParams(vmem_limit_bytes=14 << 20),
        name=name,
    )(*scalars, *(values for values, _ in operands))


def look_in(ids_ref):
    return lambda i: ids_ref[0, i]


def ids_of(ids, place):
    return ids, pl.BlockSpec((None, *ids.shape[1:]), lambda i, *_: (place, 0, 0), memory_space=pltpu.SMEM)


def order_ids(plan_ref, spans_ref, ids_ref, own_ids_ref, columns, rows):
    dp_count, _, count = spans_ref.shape
    blocks = columns // LANES
    per_owner = rows // dp_count * blocks
    factor = -(-(1 << 18) // blocks)
    assert per_owner * (factor * blocks - (1 << 18)) < 1 << 18
    for p in range(dp_count):
        owner = plan_ref[plan_ref.shape[0] - dp_count + p]
        spans = spans_ref[owner]
        row = lax.shift_right_logical(spans * factor, 18)
        column = spans - row * blocks
        tile = lax.shift_right_logical(row, 3) * blocks + column
        place = tile * SUBLANES + (row & 7)
        ids_ref[p, :, :count] = place + owner * per_owner
        if p == 0:
            own_ids_ref[0] = place
        ids_ref[p, :, count:] = jnp.full((1, LANES), 1, jnp.int32) * owner


def slot_of(place, tensor_count):
    if place in (0, tensor_count // 2):
        return 0 if place == 0 else tensor_count - 1
    return 2 * place if place < tensor_count // 2 else 2 * (tensor_count - place) - 1


def grad_copies(plan_ref, places, tokens, grad_ref, held_ref, sems, first=0):
    half, copies = tokens // 2, []
    for n, j in enumerate(places):
        slot = slot_of(j, held_ref.shape[0] // tokens)
        for k in range(2):
            at = pl.ds(pl.multiple_of(plan_ref[j] * tokens + k * half, half), half)
            to = pl.ds(slot * tokens + k * half, half)
            copies.append(pltpu.make_async_copy(grad_ref.at[at], held_ref.at[to], sems.at[first + 2 * n + k]))
    return copies


def load_body(places, plan_ref, residual_ref, grad_ref, own_ref, spans_ref, *refs):
    total_ref, held_ref, own_held, ids_ref, own_ids_ref, spans_held, sems, own_sems = refs
    tokens = own_ref.shape[0]
    spans_copy = pltpu.make_async_copy(spans_ref, spans_held, own_sems.at[1])
    spans_copy.start()
    copies = [pltpu.make_async_copy(own_ref, own_held, own_sems.at[0])]
    copies += split_copies(residual_ref, total_ref, 8, sems)
    copies += grad_copies(plan_ref, places, tokens, grad_ref, held_ref, sems, 8)
    start_all(copies)
    spans_copy.wait()
    order_ids(plan_ref, spans_held, ids_ref, own_ids_ref, total_ref.shape[1], total_ref.shape[0])
    wait_all(copies)


def load(plan, residual, token_grad, own, spans, places):
    dp_count, _, count = spans.shape
    return call(
        functools.partial(load_body, places),
        "load",
        [plan],
        [(away(residual), False), (away(token_grad), False), (away(own), False), (away(spans), False)],
        [
            (residual.shape, jnp.float32, True),
            (token_grad.shape, token_grad.dtype, True),
            (own.shape, own.dtype, True),
            ((dp_count, 1, count + LANES), jnp.int32, True),
            ((1, 1, count), jnp.int32, True),
        ],
        [pltpu.VMEM(spans.shape, jnp.int32), DMA((8 + 2 * len(places),)), DMA((2,))],
        flops=WEIGHT * own.size * residual.shape[1],
        traffic=WEIGHT * residual.size,
    )


def accumulate_body(places, coming, tokens, side, plan_ref, total_in, held_in, grad_ref, *refs):
    chunks, refs = refs[: len(places)], refs[len(places) :]
    starts = [slot_of(j, held_in.shape[0] // tokens) * tokens for j in places]
    extra = {"states": 3, "params": 1, "pick": 4}.get(side, 0)
    sources, (total_out, held_ref), refs = refs[:extra], refs[extra : extra + 2], refs[extra + 2 :]
    sems = refs[-1]
    copies = grad_copies(plan_ref, coming, tokens, grad_ref, held_ref, sems, 6)
    if side == "states":
        helds = refs[:3]
        copies += [c for n in range(3) for c in split_copies(sources[n], helds[n], 2, sems, 2 * n)]
    if side == "params":
        wide_ref, narrow_ref = refs[:2]
        copies += split_copies(sources[0], narrow_ref, 4, sems)
    start_all(copies)
    beside = None
    if side == "pick":

        def beside(i, steps):
            share = refs[0].shape[0] // steps
            for first in range(0, share, UNROLL):
                rows = [i * share + first + k for k in range(UNROLL)]
                at = [sources[3][0, row] for row in rows]
                for source, target in zip(sources[:3], refs[:3]):
                    values = [source[pl.ds(a, 1), :] for a in at]
                    for row, value in zip(rows, values):
                        target[pl.ds(row, 1), :] = value

    add_products(total_in, total_out, held_ref, list(zip(chunks, starts)), beside)
    wait_all(copies)
    if side == "params":
        wide_ref[...] = narrow_ref[...].astype(jnp.float32)


def accumulate(plan, total, chunks, places, held_grad, token_grad, coming, side=None, sources=()):
    tokens = chunks[0].shape[0]
    outs, scratch = [(total.shape, jnp.float32, True), (held_grad.shape, held_grad.dtype, True)], []
    inputs = []
    if side == "states":
        inputs = [(away(v), False) for v in sources]
        outs += [(sources[0].shape, jnp.float32, True)] * 3
    if side == "pick":
        count = sources[3][0].shape[2]
        inputs = [(v, True) for v in sources[:3]] + [sources[3]]
        outs += [((count, LANES), jnp.float32, True)] * 3
    if side == "params":
        inputs = [(away(sources[0]), False)]
        outs += [(sources[0].shape, jnp.float32, True)]
        scratch = [pltpu.VMEM(sources[0].shape, sources[0].dtype)]
    return call(
        functools.partial(accumulate_body, places, coming, tokens, side),
        "accumulate",
        [plan],
        [(total, True), (held_grad, True), (away(token_grad), False)] + [(c, True) for c in chunks] + inputs,
        outs,
        scratch + [DMA((6 + 2 * len(coming),))],
        {0: 0, 1: 1},
        flops=WEIGHT * tokens * total.size * len(chunks),
        traffic=WEIGHT * total.size,
    )


def last_body(total_in, grad_ref, front_ref, back_ref, total_out, chunk_ref):
    half = front_ref.shape[0]
    chunk_ref[:half] = front_ref[...]
    chunk_ref[half:] = back_ref[...]
    add_products(total_in, total_out, grad_ref, [(chunk_ref, grad_ref.shape[0] - 2 * half)])


def last(total, front, back, held_grad):
    half, rows = front.shape
    return call(
        last_body,
        "last",
        [],
        [(total, True), (held_grad, True), (front, True), (back, True)],
        [(total.shape, jnp.float32, True)],
        [pltpu.VMEM((2 * half, rows), front.dtype)],
        {0: 0},
        flops=4 * half * total.size,
        traffic=8 * total.size,
    )[0]


def pack_body(ids_ref, total_ref, *refs):
    packed_ref, rows_ref = refs[-2:]
    if packed_ref.dtype == jnp.float32:
        gather_rows(look_in(ids_ref), packed_ref.shape[0], [(total_ref, packed_ref)])
    else:
        gather_rows(look_in(ids_ref), packed_ref.shape[0], [(total_ref, rows_ref)])
        packed_ref[...] = rows_ref[...].astype(packed_ref.dtype)


def pack(ids, total, place, kind, after=()):
    shape = (ids.shape[2] - LANES, LANES)
    return call(
        pack_body,
        "pack",
        [],
        [ids_of(ids, place), (total, True)] + [(v, True) for v in after],
        [(shape, kind, True)],
        [pltpu.VMEM(shape, jnp.float32)],
        traffic=40 * shape[0] * LANES,
    )[0]


def clear(ids_ref, total_ref):
    zero = jnp.zeros((1, LANES), jnp.float32)

    def body(rows):
        for at in [ids_ref[0, i] for i in rows]:
            total_ref[pl.ds(at, 1), :] = zero

    each_group(ids_ref.shape[1] - LANES, body)


def close_body(others, own_ids, *refs):
    total_ref, packed_ref = refs[-2:]
    gather_rows(look_in(own_ids), packed_ref.shape[0], [(total_ref, packed_ref)])
    for ids_ref in (own_ids, *refs[:others]):
        clear(ids_ref, total_ref)


def close(ids, total, place, others, after):
    return call(
        functools.partial(close_body, len(others)),
        "close",
        [],
        [ids_of(ids, p) for p in (place, *others)] + [(total, True)] + [(v, True) for v in after],
        [(total.shape, jnp.float32, True), ((ids.shape[2] - LANES, LANES), jnp.float32, True)],
        (),
        {1 + len(others): 0},
        traffic=total.size // 4,
    )


def spread_one(ids_ref, update_ref, wide_ref, out_ref, rows_ref, block_ref, sems, first):
    per_owner, count = block_ref.shape[0], update_ref.shape[0]
    at = pl.ds(pl.multiple_of(ids_ref[0, count] * per_owner, 2 * SUBLANES), per_owner)
    rows_ref[...] = update_ref[...].astype(jnp.float32)
    scatter_rows(look_in(ids_ref), count, [(rows_ref, wide_ref)])
    return narrow(wide_ref.at[at], block_ref, out_ref.at[at], sems, first)


def narrow(source, block_ref, target, sems, first):
    copies = split_copies(block_ref, target, PARTS, sems, first)
    size = block_ref.shape[0] // PARTS
    for k, copy in enumerate(copies):
        block_ref[k * size : (k + 1) * size, :] = source[k * size : (k + 1) * size, :].astype(block_ref.dtype)
        copy.start()
    return copies


def store_body(dp_count, own_ids_ref, ids_ref, total_ref, *refs):
    new, update_ref, refs = refs[3:6], refs[7], refs[8:]
    helds, wide_ref, residual_ref, outs, out_ref = refs[:3], refs[3], refs[4], refs[5:8], refs[8]
    rows_ref, block_ref, sems = refs[9:]
    per_owner, count = block_ref.shape[0], update_ref.shape[0]
    copies = split_copies(total_ref, residual_ref, 2 * dp_count, sems)
    start_all(copies)
    mine = pl.ds(pl.multiple_of(ids_ref[0, 0] * per_owner, 2 * SUBLANES), per_owner)
    rows_ref[...] = update_ref[...].astype(jnp.float32)
    scatter_rows(look_in(own_ids_ref), count, [*zip(new, helds), (rows_ref, wide_ref.at[mine])])
    for held, out in zip(helds, outs):
        copies += split_copies(held, out, 2, sems, len(copies))
        start_all(copies[-2:])
    copies += narrow(wide_ref.at[mine], block_ref, out_ref.at[mine], sems, len(copies))
    wait_all(copies)


def store(ids, own_ids, total, helds, updates, wide, rounded):
    size, count, dp_count = helds[0].shape, own_ids.shape[2], ids.shape[0]
    owner = pl.BlockSpec((None, 1, LANES), lambda i: (0, 0, count // LANES), memory_space=pltpu.SMEM)
    if count % LANES:
        owner = pl.BlockSpec((None, 1, LANES), lambda i: (0, 0, 0), memory_space=pltpu.SMEM)
        ids = ids[:, :, count:]
    out = call(
        functools.partial(store_body, dp_count),
        "store",
        [],
        [ids_of(own_ids, 0), (ids, owner)] + [(v, True) for v in [total, *helds, *updates, wide, rounded]],
        [(size, jnp.float32, True)] * 3
        + [(wide.shape, jnp.float32, True), (total.shape, jnp.float32, False)]
        + [(size, jnp.float32, False)] * 3
        + [(wide.shape, rounded.dtype, False)],
        [pltpu.VMEM((count, LANES), jnp.float32), pltpu.VMEM(size, rounded.dtype), DMA((6 + PARTS + 2 * dp_count,))],
        {3: 0, 4: 1, 5: 2, 9: 3},
        traffic=4 * WEIGHT * size[0] * LANES,
    )
    return out[4], out[5:8], out[3], out[8]


def relay(values, after):
    return call(
        lambda *_: None,
        "relay",
        [],
        [(values, True), after],
        [(values.shape, values.dtype, True)],
        (),
        {0: 0},
    )[0]


def spread_body(count, *refs):
    ids, updates = refs[:count], refs[count + 1 : 2 * count + 1]
    wide_ref, out_ref, rows_ref, blocks_ref, sems = refs[2 * count + 2 :]
    copies = []
    for n in range(count):
        copies += spread_one(ids[n], updates[n], wide_ref, out_ref, rows_ref, blocks_ref.at[n], sems, PARTS * n)
    wait_all(copies)


def spread(ids, wide, earlier, updates, places):
    dp_count, n = ids.shape[0], len(places)
    kind = updates[0].dtype
    return call(
        functools.partial(spread_body, n),
        "spread",
        [],
        [ids_of(ids, place) for place in places] + [(wide, True)] + [(v, True) for v in updates] + [(earlier, False)],
        [(wide.shape, jnp.float32, True), (wide.shape, kind, False)],
        [
            pltpu.VMEM(updates[0].shape, jnp.float32),
            pltpu.VMEM((n, wide.shape[0] // dp_count, LANES), kind),
            DMA((PARTS * n,)),
        ],
        {n: 0, 1 + 2 * n: 1},
        traffic=WEIGHT * wide.size,
    )


def local(table, ring, activations, out_grad, residual, chosen, master, moment_one, moment_two, params):
    token_grad = out_grad[0]
    own = activations[0]
    tokens, row_count = own.shape
    column_count = token_grad.shape[1]
    dp_count, tensor_count = table.shape[:2]
    chips = dp_count // 2
    owner_rows = row_count // dp_count

    plan = jnp.asarray(table)[lax.axis_index("dp"), lax.axis_index("tensor")]
    ahead = [(ring[i], ring[(i + 1) % tensor_count]) for i in range(tensor_count)]
    behind = [(b, a) for a, b in ahead]

    def place_of(k, j):
        return 2 * k + j

    def swap(values):
        return lax.ppermute(values, "dp", [(d, d ^ 1) for d in range(dp_count)])

    def send(values, k):
        return lax.ppermute(values, "dp", [(d, ((d // 2 + k) % chips) * 2 + d % 2) for d in range(dp_count)])

    own_place = place_of(0, 0)
    states = [tiles(v) for v in (moment_one, moment_two, master)]
    front, back = lax.ppermute(own, "tensor", ahead), lax.ppermute(own, "tensor", behind)
    def chunks_of(hop):
        return [tensor_count - hop, hop] if hop < tensor_count // 2 else [hop]

    total, held_grad, own, ids, own_ids = load(plan, residual[0], token_grad, own, chosen, [0, *chunks_of(1)])
    for hop in range(1, tensor_count // 2):
        chunks, places = [front, back], chunks_of(hop)
        if hop == 1:
            chunks, places = [own, *chunks], [0, *places]
        if hop == tensor_count // 2 - 1:
            front, back = front[: tokens // 2], back[tokens // 2 :]
        front, back = lax.ppermute(front, "tensor", ahead), lax.ppermute(back, "tensor", behind)
        side, sources = None, ()
        if hop == tensor_count // 2 - 1:
            side, sources = "pick", [*helds, ids_of(own_ids, 0)]
        elif hop == 1:
            side, sources = "states", states
        elif hop == 2:
            side, sources = "params", [tiles(params)]
        total, held_grad, *fetched = accumulate(
            plan, total, chunks, places, held_grad, token_grad, chunks_of(hop + 1), side, sources
        )
        if side == "states":
            helds = fetched
        if side == "params":
            (wide,) = fetched
        if side == "pick":
            picked = fetched
    total = tiles(last(total, front, back, held_grad))

    received, sums = [], []
    for k in range(1, chips):
        other = swap(pack(ids, total, place_of(k, 1), jnp.bfloat16))
        mine = pack(ids, total, place_of(k, 0), jnp.float32)
        sums.append((mine + other.astype(jnp.float32)).astype(jnp.bfloat16))
        received.append(send(sums[-1], k))
    other = pack(ids, total, place_of(0, 1), jnp.bfloat16, sums)
    received.append(swap(other))
    total, mine = close(ids, total, own_place, range(1, dp_count), [*sums, other])
    received[0] = relay(received[0], (mine, True))
    for part in received:
        mine = mine + part.astype(jnp.float32)
    mean_grad = mine / dp_count

    one, two, weights = picked
    one = beta_one * one + (1.0 - beta_one) * mean_grad
    two = beta_two * two + (1.0 - beta_two) * mean_grad * mean_grad
    weights = weights - learn_rate * (one / (jnp.sqrt(two) + epsilon) + decay_rate * weights)
    rounded = weights.astype(jnp.bfloat16)

    far = [send(rounded, k) for k in range(1, chips)]
    near = swap(rounded)
    new_residual, fresh, wide, out = store(
        ids, own_ids, total, helds, [one, two, weights], wide, rounded
    )
    for k in range(1, chips):
        direct = relay(far[k - 1], (away(out), False))
        across = swap(direct)
        updates, places = [direct], [place_of(chips - k, 0)]
        if k == 1:
            updates, places = [near, *updates], [place_of(0, 1), *places]
        wide, out = spread(ids, wide, out, updates, places)
        wide, out = spread(ids, wide, out, [across], [place_of(chips - k, 1)])

    new_one, new_two, new_master = (untiles(v, owner_rows, column_count) for v in fresh)
    return (
        untiles(new_residual, row_count, column_count)[None],
        new_one,
        new_two,
        new_master,
        untiles(out, row_count, column_count),
    )


def solution(mesh):
    dp_count, tensor_count = mesh.shape["dp"], mesh.shape["tensor"]
    body = functools.partial(local, plan_table(dp_count, tensor_count), ring_order(tensor_count))
    in_specs = (
        P("dp", "tensor", None),
        P("dp", None, "tensor"),
        P("dp", None, "tensor"),
        P(None, "tensor", None),
        P("dp", "tensor"),
        P("dp", "tensor"),
        P("dp", "tensor"),
        P(None, "tensor"),
    )
    out_specs = (
        P("dp", None, "tensor"),
        P("dp", "tensor"),
        P("dp", "tensor"),
        P("dp", "tensor"),
        P(None, "tensor"),
    )
    return jax.shard_map(body, mesh=mesh, in_specs=in_specs, out_specs=out_specs, check_vma=False)
```

```python
import functools
import jax
import jax.numpy as jnp
import numpy as np
from jax import lax
from jax.experimental import pallas as pl
from jax.experimental.pallas import tpu as pltpu
from jax.sharding import PartitionSpec as P

beta_one = 0.9
beta_two = 0.999
learn_rate = 0.01
decay_rate = 0.1
epsilon = 1e-08
LANES = 128
SUBLANES = 8
UNROLL = 32
GROUP = 8


def ring_order(count):
    inner = 4 if count % 16 == 0 else 2
    outer = count // inner
    cells = []
    for row in range(outer):
        steps = range(1, inner) if row % 2 == 0 else range(inner - 1, 0, -1)
        cells += [row * inner + step for step in steps]
    return cells + [row * inner for row in range(outer - 1, -1, -1)]


def plan_table(dp_count, tensor_count):
    ring = ring_order(tensor_count)
    place = {cell: i for i, cell in enumerate(ring)}
    chips = dp_count // 2
    table = np.zeros((dp_count, tensor_count, tensor_count + dp_count), np.int32)
    for d in range(dp_count):
        owners = [((d // 2 + k) % chips) * 2 + ((d % 2) ^ j) for k in range(chips) for j in range(2)]
        for t in range(tensor_count):
            table[d, t, :tensor_count] = [ring[(place[t] + j) % tensor_count] for j in range(tensor_count)]
            table[d, t, tensor_count:] = owners
    return table


def tiles(values):
    rows, columns = values.shape
    split = values.reshape(rows // SUBLANES, SUBLANES, columns // LANES, LANES)
    return split.transpose(0, 2, 1, 3).reshape(rows * columns // LANES, LANES)


def untiles(values, rows, columns):
    split = values.reshape(rows // SUBLANES, columns // LANES, SUBLANES, LANES)
    return split.transpose(0, 2, 1, 3).reshape(rows, columns)


VMEM = pltpu.MemorySpace.VMEM
HELD = pl.BlockSpec(memory_space=VMEM)
AWAY = pl.BlockSpec(memory_space=pl.ANY)
DMA = pltpu.SemaphoreType.DMA
WIDTH = 1792
WEIGHT = 24
PARTS = 4


def each_group(count, body):
    def step(i, carry):
        body([i * UNROLL + k for k in range(UNROLL)])
        return carry

    lax.fori_loop(0, count // UNROLL, step, 0)


def gather_rows(look, count, pairs):
    def move(rows):
        at = [look(i) for i in rows]
        for source, target in pairs:
            values = [source[pl.ds(a, 1), :] for a in at]
            for i, value in zip(rows, values):
                target[pl.ds(i, 1), :] = value

    each_group(count, move)


def scatter_rows(look, count, pairs):
    def move(rows):
        at = [look(i) for i in rows]
        for source, target in pairs:
            values = [source[pl.ds(i, 1), :] for i in rows]
            for a, value in zip(at, values):
                target[pl.ds(a, 1), :] = value

    each_group(count, move)


def product(a, b):
    return lax.dot_general(a, b, (((0,), (0,)), ((), ())), preferred_element_type=jnp.float32)


def add_products(total_in, total_out, grad_ref, terms, beside=None):
    columns = grad_ref.shape[1]
    width = WIDTH if columns % WIDTH == 0 else LANES

    def step(i, carry):
        at = pl.ds(pl.multiple_of(i * width, LANES), width)
        total = total_in[:, at]
        for chunk, start in terms:
            total = total + product(chunk[...], grad_ref[pl.ds(start, chunk.shape[0]), at])
        total_out[:, at] = total
        if beside is not None:
            beside(i, columns // width)
        return carry

    lax.fori_loop(0, columns // width, step, 0)


def split_copies(source, target, parts, sems, first=0):
    size = source.shape[0] // parts
    return [
        pltpu.make_async_copy(source.at[pl.ds(k * size, size)], target.at[pl.ds(k * size, size)], sems.at[first + k])
        for k in range(parts)
    ]


def start_all(copies):
    for copy in copies:
        copy.start()


def wait_all(copies):
    for copy in copies:
        copy.wait()


def away(values):
    return pltpu.with_memory_space_constraint(values, pltpu.MemorySpace.HBM)


def call(body, name, scalars, operands, outs, scratch=(), aliases=None, flops=0, traffic=0):
    return pl.pallas_call(
        body,
        out_shape=[
            pltpu.VMEM(shape, kind) if held else jax.ShapeDtypeStruct(shape, kind) for shape, kind, held in outs
        ],
        grid_spec=pltpu.PrefetchScalarGridSpec(
            num_scalar_prefetch=len(scalars),
            grid=(1,),
            in_specs=[held if isinstance(held, pl.BlockSpec) else HELD if held else AWAY for _, held in operands],
            out_specs=[HELD if held else AWAY for _, _, held in outs],
            scratch_shapes=list(scratch),
        ),
        input_output_aliases={len(scalars) + k: v for k, v in (aliases or {}).items()},
        cost_estimate=pl.CostEstimate(flops=flops, bytes_accessed=traffic, transcendentals=0),
        compiler_params=pltpu.CompilerParams(vmem_limit_bytes=14 << 20),
        name=name,
    )(*scalars, *(values for values, _ in operands))


def look_in(ids_ref):
    return lambda i: ids_ref[0, i]


def ids_of(ids, place):
    return ids, pl.BlockSpec((None, *ids.shape[1:]), lambda i, *_: (place, 0, 0), memory_space=pltpu.SMEM)


def order_ids(plan_ref, spans_ref, ids_ref, own_ids_ref, columns, rows):
    dp_count, _, count = spans_ref.shape
    blocks = columns // LANES
    per_owner = rows // dp_count * blocks
    factor = -(-(1 << 18) // blocks)
    assert per_owner * (factor * blocks - (1 << 18)) < 1 << 18
    for p in range(dp_count):
        owner = plan_ref[plan_ref.shape[0] - dp_count + p]
        spans = spans_ref[owner]
        row = lax.shift_right_logical(spans * factor, 18)
        column = spans - row * blocks
        tile = lax.shift_right_logical(row, 3) * blocks + column
        place = tile * SUBLANES + (row & 7)
        ids_ref[p, :, :count] = place + owner * per_owner
        if p == 0:
            own_ids_ref[0] = place
        ids_ref[p, :, count:] = jnp.full((1, LANES), 1, jnp.int32) * owner


def slot_of(place, tensor_count):
    if place in (0, tensor_count // 2):
        return 0 if place == 0 else tensor_count - 1
    return 2 * place if place < tensor_count // 2 else 2 * (tensor_count - place) - 1


def grad_copies(plan_ref, places, tokens, grad_ref, held_ref, sems, first=0):
    half, copies = tokens // 2, []
    for n, j in enumerate(places):
        slot = slot_of(j, held_ref.shape[0] // tokens)
        for k in range(2):
            at = pl.ds(pl.multiple_of(plan_ref[j] * tokens + k * half, half), half)
            to = pl.ds(slot * tokens + k * half, half)
            copies.append(pltpu.make_async_copy(grad_ref.at[at], held_ref.at[to], sems.at[first + 2 * n + k]))
    return copies


def load_body(places, plan_ref, residual_ref, grad_ref, own_ref, spans_ref, *refs):
    total_ref, held_ref, own_held, ids_ref, own_ids_ref, spans_held, sems, own_sems = refs
    tokens = own_ref.shape[0]
    spans_copy = pltpu.make_async_copy(spans_ref, spans_held, own_sems.at[1])
    spans_copy.start()
    copies = [pltpu.make_async_copy(own_ref, own_held, own_sems.at[0])]
    copies += split_copies(residual_ref, total_ref, 8, sems)
    copies += grad_copies(plan_ref, places, tokens, grad_ref, held_ref, sems, 8)
    start_all(copies)
    spans_copy.wait()
    order_ids(plan_ref, spans_held, ids_ref, own_ids_ref, total_ref.shape[1], total_ref.shape[0])
    wait_all(copies)


def load(plan, residual, token_grad, own, spans, places):
    dp_count, _, count = spans.shape
    return call(
        functools.partial(load_body, places),
        "load",
        [plan],
        [(away(residual), False), (away(token_grad), False), (away(own), False), (away(spans), False)],
        [
            (residual.shape, jnp.float32, True),
            (token_grad.shape, token_grad.dtype, True),
            (own.shape, own.dtype, True),
            ((dp_count, 1, count + LANES), jnp.int32, True),
            ((1, 1, count), jnp.int32, True),
        ],
        [pltpu.VMEM(spans.shape, jnp.int32), DMA((8 + 2 * len(places),)), DMA((2,))],
        flops=WEIGHT * own.size * residual.shape[1],
        traffic=WEIGHT * residual.size,
    )


def accumulate_body(places, coming, tokens, side, plan_ref, total_in, held_in, grad_ref, *refs):
    chunks, refs = refs[: len(places)], refs[len(places) :]
    starts = [slot_of(j, held_in.shape[0] // tokens) * tokens for j in places]
    extra = {"states": 3, "params": 1, "pick": 4}.get(side, 0)
    sources, (total_out, held_ref), refs = refs[:extra], refs[extra : extra + 2], refs[extra + 2 :]
    sems = refs[-1]
    copies = grad_copies(plan_ref, coming, tokens, grad_ref, held_ref, sems, 6)
    if side == "states":
        helds = refs[:3]
        copies += [c for n in range(3) for c in split_copies(sources[n], helds[n], 2, sems, 2 * n)]
    if side == "params":
        wide_ref, narrow_ref = refs[:2]
        copies += split_copies(sources[0], narrow_ref, 4, sems)
    start_all(copies)
    beside = None
    if side == "pick":

        def beside(i, steps):
            share = refs[0].shape[0] // steps
            for first in range(0, share, GROUP):
                rows = [i * share + first + k for k in range(GROUP)]
                at = [sources[3][0, row] for row in rows]
                for source, target in zip(sources[:3], refs[:3]):
                    values = [source[pl.ds(a, 1), :] for a in at]
                    for row, value in zip(rows, values):
                        target[pl.ds(row, 1), :] = value

    add_products(total_in, total_out, held_ref, list(zip(chunks, starts)), beside)
    wait_all(copies)
    if side == "params":
        wide_ref[...] = narrow_ref[...].astype(jnp.float32)


def accumulate(plan, total, chunks, places, held_grad, token_grad, coming, side=None, sources=()):
    tokens = chunks[0].shape[0]
    outs, scratch = [(total.shape, jnp.float32, True), (held_grad.shape, held_grad.dtype, True)], []
    inputs = []
    if side == "states":
        inputs = [(away(v), False) for v in sources]
        outs += [(sources[0].shape, jnp.float32, True)] * 3
    if side == "pick":
        count = sources[3][0].shape[2]
        inputs = [(v, True) for v in sources[:3]] + [sources[3]]
        outs += [((count, LANES), jnp.float32, True)] * 3
    if side == "params":
        inputs = [(away(sources[0]), False)]
        outs += [(sources[0].shape, jnp.float32, True)]
        scratch = [pltpu.VMEM(sources[0].shape, sources[0].dtype)]
    return call(
        functools.partial(accumulate_body, places, coming, tokens, side),
        "accumulate",
        [plan],
        [(total, True), (held_grad, True), (away(token_grad), False)] + [(c, True) for c in chunks] + inputs,
        outs,
        scratch + [DMA((6 + 2 * len(coming),))],
        {0: 0, 1: 1},
        flops=WEIGHT * tokens * total.size * len(chunks),
        traffic=WEIGHT * total.size,
    )


def last_body(total_in, grad_ref, front_ref, back_ref, total_out, chunk_ref):
    half = front_ref.shape[0]
    chunk_ref[:half] = front_ref[...]
    chunk_ref[half:] = back_ref[...]
    add_products(total_in, total_out, grad_ref, [(chunk_ref, grad_ref.shape[0] - 2 * half)])


def last(total, front, back, held_grad):
    half, rows = front.shape
    return call(
        last_body,
        "last",
        [],
        [(total, True), (held_grad, True), (front, True), (back, True)],
        [(total.shape, jnp.float32, True)],
        [pltpu.VMEM((2 * half, rows), front.dtype)],
        {0: 0},
        flops=4 * half * total.size,
        traffic=8 * total.size,
    )[0]


def pack_body(ids_ref, total_ref, *refs):
    packed_ref, rows_ref = refs[-2:]
    if packed_ref.dtype == jnp.float32:
        gather_rows(look_in(ids_ref), packed_ref.shape[0], [(total_ref, packed_ref)])
    else:
        gather_rows(look_in(ids_ref), packed_ref.shape[0], [(total_ref, rows_ref)])
        packed_ref[...] = rows_ref[...].astype(packed_ref.dtype)


def pack(ids, total, place, kind, after=()):
    shape = (ids.shape[2] - LANES, LANES)
    return call(
        pack_body,
        "pack",
        [],
        [ids_of(ids, place), (total, True)] + [(v, True) for v in after],
        [(shape, kind, True)],
        [pltpu.VMEM(shape, jnp.float32)],
        traffic=40 * shape[0] * LANES,
    )[0]


def clear(ids_ref, total_ref):
    zero = jnp.zeros((1, LANES), jnp.float32)

    def body(rows):
        for at in [ids_ref[0, i] for i in rows]:
            total_ref[pl.ds(at, 1), :] = zero

    each_group(ids_ref.shape[1] - LANES, body)


def close_body(others, own_ids, *refs):
    total_ref, packed_ref = refs[-2:]
    gather_rows(look_in(own_ids), packed_ref.shape[0], [(total_ref, packed_ref)])
    for ids_ref in (own_ids, *refs[:others]):
        clear(ids_ref, total_ref)


def close(ids, total, place, others, after):
    return call(
        functools.partial(close_body, len(others)),
        "close",
        [],
        [ids_of(ids, p) for p in (place, *others)] + [(total, True)] + [(v, True) for v in after],
        [(total.shape, jnp.float32, True), ((ids.shape[2] - LANES, LANES), jnp.float32, True)],
        (),
        {1 + len(others): 0},
        traffic=total.size // 4,
    )


def spread_one(ids_ref, update_ref, wide_ref, out_ref, rows_ref, block_ref, sems, first):
    per_owner, count = block_ref.shape[0], update_ref.shape[0]
    at = pl.ds(pl.multiple_of(ids_ref[0, count] * per_owner, 2 * SUBLANES), per_owner)
    rows_ref[...] = update_ref[...].astype(jnp.float32)
    scatter_rows(look_in(ids_ref), count, [(rows_ref, wide_ref)])
    return narrow(wide_ref.at[at], block_ref, out_ref.at[at], sems, first)


def narrow(source, block_ref, target, sems, first):
    copies = split_copies(block_ref, target, PARTS, sems, first)
    size = block_ref.shape[0] // PARTS
    for k, copy in enumerate(copies):
        block_ref[k * size : (k + 1) * size, :] = source[k * size : (k + 1) * size, :].astype(block_ref.dtype)
        copy.start()
    return copies


def store_body(dp_count, own_ids_ref, ids_ref, total_ref, *refs):
    new, update_ref, refs = refs[3:6], refs[7], refs[8:]
    helds, wide_ref, residual_ref, outs, out_ref = refs[:3], refs[3], refs[4], refs[5:8], refs[8]
    rows_ref, block_ref, sems = refs[9:]
    per_owner, count = block_ref.shape[0], update_ref.shape[0]
    copies = split_copies(total_ref, residual_ref, 2 * dp_count, sems)
    start_all(copies)
    mine = pl.ds(pl.multiple_of(ids_ref[0, 0] * per_owner, 2 * SUBLANES), per_owner)
    rows_ref[...] = update_ref[...].astype(jnp.float32)
    scatter_rows(look_in(own_ids_ref), count, [*zip(new, helds), (rows_ref, wide_ref.at[mine])])
    for held, out in zip(helds, outs):
        copies += split_copies(held, out, 2, sems, len(copies))
        start_all(copies[-2:])
    copies += narrow(wide_ref.at[mine], block_ref, out_ref.at[mine], sems, len(copies))
    wait_all(copies)


def store(ids, own_ids, total, helds, updates, wide, rounded):
    size, count, dp_count = helds[0].shape, own_ids.shape[2], ids.shape[0]
    owner = pl.BlockSpec((None, 1, LANES), lambda i: (0, 0, count // LANES), memory_space=pltpu.SMEM)
    if count % LANES:
        owner = pl.BlockSpec((None, 1, LANES), lambda i: (0, 0, 0), memory_space=pltpu.SMEM)
        ids = ids[:, :, count:]
    out = call(
        functools.partial(store_body, dp_count),
        "store",
        [],
        [ids_of(own_ids, 0), (ids, owner)] + [(v, True) for v in [total, *helds, *updates, wide, rounded]],
        [(size, jnp.float32, True)] * 3
        + [(wide.shape, jnp.float32, True), (total.shape, jnp.float32, False)]
        + [(size, jnp.float32, False)] * 3
        + [(wide.shape, rounded.dtype, False)],
        [pltpu.VMEM((count, LANES), jnp.float32), pltpu.VMEM(size, rounded.dtype), DMA((6 + PARTS + 2 * dp_count,))],
        {3: 0, 4: 1, 5: 2, 9: 3},
        traffic=4 * WEIGHT * size[0] * LANES,
    )
    return out[4], out[5:8], out[3], out[8]


def relay(values, after):
    return call(
        lambda *_: None,
        "relay",
        [],
        [(values, True), after],
        [(values.shape, values.dtype, True)],
        (),
        {0: 0},
    )[0]


def spread_body(count, *refs):
    ids, updates = refs[:count], refs[count + 1 : 2 * count + 1]
    wide_ref, out_ref, rows_ref, blocks_ref, sems = refs[2 * count + 2 :]
    copies = []
    for n in range(count):
        copies += spread_one(ids[n], updates[n], wide_ref, out_ref, rows_ref, blocks_ref.at[n], sems, PARTS * n)
    wait_all(copies)


def spread(ids, wide, earlier, updates, places):
    dp_count, n = ids.shape[0], len(places)
    kind = updates[0].dtype
    return call(
        functools.partial(spread_body, n),
        "spread",
        [],
        [ids_of(ids, place) for place in places] + [(wide, True)] + [(v, True) for v in updates] + [(earlier, False)],
        [(wide.shape, jnp.float32, True), (wide.shape, kind, False)],
        [
            pltpu.VMEM(updates[0].shape, jnp.float32),
            pltpu.VMEM((n, wide.shape[0] // dp_count, LANES), kind),
            DMA((PARTS * n,)),
        ],
        {n: 0, 1 + 2 * n: 1},
        traffic=WEIGHT * wide.size,
    )


def local(table, ring, activations, out_grad, residual, chosen, master, moment_one, moment_two, params):
    token_grad = out_grad[0]
    own = activations[0]
    tokens, row_count = own.shape
    column_count = token_grad.shape[1]
    dp_count, tensor_count = table.shape[:2]
    chips = dp_count // 2
    owner_rows = row_count // dp_count

    plan = jnp.asarray(table)[lax.axis_index("dp"), lax.axis_index("tensor")]
    ahead = [(ring[i], ring[(i + 1) % tensor_count]) for i in range(tensor_count)]
    behind = [(b, a) for a, b in ahead]

    def place_of(k, j):
        return 2 * k + j

    def swap(values):
        return lax.ppermute(values, "dp", [(d, d ^ 1) for d in range(dp_count)])

    def send(values, k):
        return lax.ppermute(values, "dp", [(d, ((d // 2 + k) % chips) * 2 + d % 2) for d in range(dp_count)])

    own_place = place_of(0, 0)
    states = [tiles(v) for v in (moment_one, moment_two, master)]
    front, back = lax.ppermute(own, "tensor", ahead), lax.ppermute(own, "tensor", behind)
    def chunks_of(hop):
        return [tensor_count - hop, hop] if hop < tensor_count // 2 else [hop]

    total, held_grad, own, ids, own_ids = load(plan, residual[0], token_grad, own, chosen, [0, *chunks_of(1)])
    for hop in range(1, tensor_count // 2):
        chunks, places = [front, back], chunks_of(hop)
        if hop == 1:
            chunks, places = [own, *chunks], [0, *places]
        if hop == tensor_count // 2 - 1:
            front, back = front[: tokens // 2], back[tokens // 2 :]
        front, back = lax.ppermute(front, "tensor", ahead), lax.ppermute(back, "tensor", behind)
        side, sources = None, ()
        if hop == tensor_count // 2 - 1:
            side, sources = "pick", [*helds, ids_of(own_ids, 0)]
        elif hop == 1:
            side, sources = "states", states
        elif hop == 2:
            side, sources = "params", [tiles(params)]
        total, held_grad, *fetched = accumulate(
            plan, total, chunks, places, held_grad, token_grad, chunks_of(hop + 1), side, sources
        )
        if side == "states":
            helds = fetched
        if side == "params":
            (wide,) = fetched
        if side == "pick":
            picked = fetched
    total = tiles(last(total, front, back, held_grad))

    received, sums = [], []
    for k in range(1, chips):
        other = swap(pack(ids, total, place_of(k, 1), jnp.bfloat16))
        mine = pack(ids, total, place_of(k, 0), jnp.float32)
        sums.append((mine + other.astype(jnp.float32)).astype(jnp.bfloat16))
        received.append(send(sums[-1], k))
    other = pack(ids, total, place_of(0, 1), jnp.bfloat16, sums)
    received.append(swap(other))
    total, mine = close(ids, total, own_place, range(1, dp_count), [*sums, other])
    received[0] = relay(received[0], (mine, True))
    for part in received:
        mine = mine + part.astype(jnp.float32)
    mean_grad = mine / dp_count

    one, two, weights = picked
    one = beta_one * one + (1.0 - beta_one) * mean_grad
    two = beta_two * two + (1.0 - beta_two) * mean_grad * mean_grad
    weights = weights - learn_rate * (one / (jnp.sqrt(two) + epsilon) + decay_rate * weights)
    rounded = weights.astype(jnp.bfloat16)

    far = [send(rounded, k) for k in range(1, chips)]
    near = swap(rounded)
    new_residual, fresh, wide, out = store(
        ids, own_ids, total, helds, [one, two, weights], wide, rounded
    )
    for k in range(1, chips):
        direct = relay(far[k - 1], (away(out), False))
        across = swap(direct)
        updates, places = [direct], [place_of(chips - k, 0)]
        if k == 1:
            updates, places = [near, *updates], [place_of(0, 1), *places]
        wide, out = spread(ids, wide, out, updates, places)
        wide, out = spread(ids, wide, out, [across], [place_of(chips - k, 1)])

    new_one, new_two, new_master = (untiles(v, owner_rows, column_count) for v in fresh)
    return (
        untiles(new_residual, row_count, column_count)[None],
        new_one,
        new_two,
        new_master,
        untiles(out, row_count, column_count),
    )


def solution(mesh):
    dp_count, tensor_count = mesh.shape["dp"], mesh.shape["tensor"]
    body = functools.partial(local, plan_table(dp_count, tensor_count), ring_order(tensor_count))
    in_specs = (
        P("dp", "tensor", None),
        P("dp", None, "tensor"),
        P("dp", None, "tensor"),
        P(None, "tensor", None),
        P("dp", "tensor"),
        P("dp", "tensor"),
        P("dp", "tensor"),
        P(None, "tensor"),
    )
    out_specs = (
        P("dp", None, "tensor"),
        P("dp", "tensor"),
        P("dp", "tensor"),
        P("dp", "tensor"),
        P(None, "tensor"),
    )
    return jax.shard_map(body, mesh=mesh, in_specs=in_specs, out_specs=out_specs, check_vma=False)
```
